256 devices in a mesh: mem: 16 (over y, z_hi), lat: 16 (over x, z_lo, core).
Axes of the slice: x: 4, y: 4, z: 8 (z_hi: 4, z_lo: 2; z = z_hi * 2 + z_lo), core: 2. Of those that a mesh axis runs over, the one named last changes fastest.
Arguments:
- replica_variables: float32 [16, 4, 256, 4096], P('mem', None, 'lat'), may hold values from -40 to 40, as said below
- analysis: float32 [4, 256, 4096], P(None, 'lat'), may hold values from -4 to 4
- labels: int32 [256, 32], P('lat'), may hold values from 0 to 7, as said below
- pairing: int32 [16], replicated, may hold values from 0 to 15, as said below
Outputs:
- closing_ensemble_values: float32 [16, 4, 256, 4096], P('mem', None, 'lat')
- factor: float32 [16, 8], P('mem')
The draws below stay inside these ranges and needn't reach their ends.
Inputs may be any that keep to these rules, and one draw needn't show every extreme that they name: `replica_variables`: member fields; the spread of members differs across rows and columns. `labels`: every label value occurs at least once. pairing[pairing[m]] = m and pairing[m] != m for every member m.
All inputs are finite; a program needn't handle non-finite values.
Results may differ from the reference program's by a relative error of at most 0.00015.
Values sent between devices are 32-bit elements; how exact they have to be, the bound alone decides.
No kernel may reach another device: no remote copies, remote signals or barrier semaphores. Data moves between devices by JAX's collectives and lax.ppermute only.
A program may use at most 64 MiB of HBM per device.

```python
import jax
import jax.numpy as jnp
from jax import lax

LON = 4096
TILE = 128
REGIONS = 8
STEPS = 3
MEMBERS = 16
NLAT = 256


def draw_replica_variables(key, part):
    keys = jax.random.split(key, 3)
    rows = jnp.arange(NLAT).astype(jnp.float32)
    rising = jnp.exp(jnp.log(3.0) * rows / max(NLAT - 1, 1))
    row_scale = rising * jnp.exp(jax.random.uniform(keys[0], (NLAT,), minval=0.0, maxval=1.15))
    col_scale = jnp.exp(jax.random.uniform(keys[1], (LON,), minval=0.0, maxval=1.15))
    scale = 0.05 * row_scale[:, None] * col_scale[None, :]
    base = jax.random.normal(keys[2], (MEMBERS, 4, NLAT, LON))
    return (base * scale).astype(jnp.float32)


def draw_labels(key, part):
    first_key, second_key = jax.random.split(key, 2)
    tiles = LON // TILE
    base = jax.random.randint(first_key, (NLAT * tiles,), 0, REGIONS).astype(jnp.int32)
    places = jax.random.permutation(second_key, NLAT * tiles)[:REGIONS]
    base = base.at[places].set(jnp.arange(REGIONS, dtype=jnp.int32))
    return base.reshape(NLAT, tiles).astype(jnp.int32)


def draw_pairing(key, part):
    order = jax.random.permutation(key, MEMBERS).astype(jnp.int32)
    evens = order[0::2]
    odds = order[1::2]
    partner = jnp.zeros((MEMBERS,), jnp.int32).at[evens].set(odds).at[odds].set(evens)
    return partner.astype(jnp.int32)


def level_of(rng, shape, cuts, low, high):
    gain = 1.0
    for position, blocks in cuts:
        draws = jax.random.uniform(jax.random.fold_in(jax.random.fold_in(rng, 6), position), (blocks,), jnp.float32, low / len(cuts), high / len(cuts))
        gain = gain * jnp.repeat(jnp.exp(draws), shape[position] // blocks).reshape((-1,) + (1,) * (len(shape) - 1 - position))
    return gain


def gaussian(rng, extent, scale, reach, cuts=(), held_as=jnp.bfloat16):
    loudness = level_of(rng, extent, cuts, -0.22, 0.18) if cuts else 1.0
    values = jax.random.normal(rng, extent, jnp.float32) * scale * loudness
    return jnp.minimum(jnp.maximum(values, -reach), reach).astype(held_as)


def setup_inputs(seed: int = 0) -> dict:
    key_of = jax.random.split(jax.random.key(seed), 5)
    return {
        "replica_variables": draw_replica_variables(jax.random.fold_in(key_of[4], 71), 0),
        "analysis": gaussian(key_of[1], (4, NLAT, LON), 0.5, 4.0, ((1, 16),), jnp.float32),
        "labels": draw_labels(jax.random.fold_in(key_of[4], 71), 0),
        "pairing": draw_pairing(jax.random.fold_in(key_of[4], 71), 0),
    }


grav_coef = 0.1
depth_coef = 0.1
advect_coef = 0.05
diffuse_coef = 0.05
coriolis_coef = 0.05
target_size = 0.5
small_eps = 1e-06

def diff_lon(field):
    return jnp.roll(field, -1, axis=-1) - jnp.roll(field, 1, axis=-1)

def trimmed_latitude_lines(field, have, want, offset=0):
    margin = have - want
    total = field.shape[-2]
    return field[..., margin + offset:total - margin + offset, :]

def model_step(extended, have, coriolis, height_rim):
    height = extended[:, 0]
    zonal = extended[:, 1]
    meridional = extended[:, 2]
    tracer = extended[:, 3]
    inner = have - 1
    new_height = trimmed_latitude_lines(height, have, inner) - depth_coef * (diff_lon(trimmed_latitude_lines(zonal, have, inner)) + trimmed_latitude_lines(meridional, have, inner, 1) - trimmed_latitude_lines(meridional, have, inner, -1))
    new_zonal = trimmed_latitude_lines(zonal, have, inner) + trimmed_latitude_lines(coriolis, have, inner) * trimmed_latitude_lines(meridional, have, inner) - grav_coef * diff_lon(new_height)
    padded_height, height_have = height_rim(new_height, inner)
    outer = height_have - 1
    zonal_out = trimmed_latitude_lines(new_zonal, inner, outer)
    new_meridional = trimmed_latitude_lines(meridional, have, outer) - trimmed_latitude_lines(coriolis, have, outer) * zonal_out - grav_coef * (trimmed_latitude_lines(padded_height, height_have, outer, 1) - trimmed_latitude_lines(padded_height, height_have, outer, -1))
    centre = trimmed_latitude_lines(tracer, have, outer)
    upper = trimmed_latitude_lines(tracer, have, outer, 1)
    lower = trimmed_latitude_lines(tracer, have, outer, -1)
    new_tracer = centre - advect_coef * (zonal_out * diff_lon(centre) + new_meridional * (upper - lower)) + diffuse_coef * (jnp.roll(centre, -1, axis=-1) + jnp.roll(centre, 1, axis=-1) + upper + lower - 4.0 * centre)
    quantity_bundle = jnp.stack([trimmed_latitude_lines(padded_height, height_have, outer), zonal_out, new_meridional, new_tracer], axis=1)
    return (quantity_bundle, outer)

def height_with_halo(new_height, have):
    return (jnp.pad(new_height, ((0, 0), (1, 1), (0, 0))), have + 1)

def predicted_flow(quantity_bundle):
    rows_all = quantity_bundle.shape[2]
    global_rows = jnp.arange(-1, rows_all + 1).astype(jnp.float32)
    coriolis = (coriolis_coef * (2.0 * (global_rows + 0.5) / rows_all - 1.0))[:, None]
    for index in range(STEPS):
        extended = jnp.pad(quantity_bundle, ((0, 0), (0, 0), (1, 1), (0, 0)))
        quantity_bundle, _ = model_step(extended, 1, coriolis, height_with_halo)
    return quantity_bundle

def reference(replica_variables, analysis, labels, pairing):
    leading_replica = predicted_flow(replica_variables)
    partner = leading_replica[pairing]
    spread = 0.5 * (leading_replica - partner)
    energy = 0.5 * lax.optimization_barrier(jnp.sum(spread * spread, axis=1))
    padded = jnp.pad(energy, ((0, 0), (1, 1), (0, 0)))
    smoothed_field = 0.25 * (padded[:, 2:] + 2.0 * energy + padded[:, :-2])
    members, rows_all, width = smoothed_field.shape
    tiles = width // TILE
    tile_sums = smoothed_field.reshape(members, rows_all, tiles, TILE).sum(-1)
    onehot = (labels[..., None] == jnp.arange(REGIONS, dtype=jnp.int32)).astype(jnp.float32)
    region_sum = jnp.einsum('mrt,rtk->mk', tile_sums, onehot, precision=lax.Precision.HIGHEST)
    cells = onehot.sum((0, 1)) * TILE
    factor = target_size / jnp.sqrt(region_sum / cells + small_eps)
    cell_factor = jnp.einsum('mk,rtk->mrt', factor, onehot, precision=lax.Precision.HIGHEST)
    scaled = (spread.reshape(members, 4, rows_all, tiles, TILE) * cell_factor[:, None, :, :, None]).reshape(spread.shape)
    central_latitude_lines = analysis[None] + scaled
    closing_ensemble_values = predicted_flow(central_latitude_lines)
    return (closing_ensemble_values, factor)
```

```python
import jax
import jax.numpy as jnp
from jax import lax
from jax.sharding import PartitionSpec as P

TILE = 128
REGIONS = 8
STEPS = 3
EDGE = 8


grav_coef = 0.1
depth_coef = 0.1
advect_coef = 0.05
diffuse_coef = 0.05
coriolis_coef = 0.05
target_size = 0.5
small_eps = 1e-06


def neighbours(axis):
    size = lax.axis_size(axis)
    up = [(i, i + 1) for i in range(size - 1)]
    return up, [(j, i) for i, j in up]


def edges(array, dim):
    up, down = neighbours("lat")
    length = array.shape[dim]
    last = lax.slice_in_dim(array, length - EDGE, length, axis=dim)
    initial = lax.slice_in_dim(array, 0, EDGE, axis=dim)
    return lax.ppermute(last, "lat", up), lax.ppermute(initial, "lat", down)


def east(field):
    return jnp.roll(field, -1, axis=-1)


def west(field):
    return jnp.roll(field, 1, axis=-1)


def step(fields, rows):
    h, u, v, q = fields
    total_rows = lax.axis_size("lat") * 16
    inside = ((rows >= 0) & (rows < total_rows)).astype(jnp.float32)[:, None]
    f = (coriolis_coef * (2.0 * (rows.astype(jnp.float32) + 0.5) / total_rows - 1.0))[:, None]
    c1 = slice(1, -1)
    h1 = (h[c1] - depth_coef * (east(u[c1]) - west(u[c1]) + v[2:] - v[:-2])) * inside[c1]
    c2 = slice(2, -2)
    ins = inside[c2]
    h1c = h1[c1]
    u1 = (u[c2] + f[c2] * v[c2] - grav_coef * (east(h1c) - west(h1c))) * ins
    v1 = (v[c2] - f[c2] * u1 - grav_coef * (h1[2:] - h1[:-2])) * ins
    qc, qn, qs = q[c2], q[3:-1], q[1:-3]
    qe, qw = east(qc), west(qc)
    q1 = (
        qc
        - advect_coef * (u1 * (qe - qw) + v1 * (qn - qs))
        + diffuse_coef * (qe + qw + qn + qs - 4.0 * qc)
    ) * ins
    return (h1c, u1, v1, q1), rows[c2]


def flow(before, middle, after):
    local_rows = middle.shape[1]
    rows = lax.axis_index("lat") * local_rows - EDGE + jnp.arange(local_rows + 2 * EDGE)
    ext = jnp.concatenate([before, middle, after], axis=1)
    fields = tuple(ext[i] for i in range(4))
    for _ in range(STEPS):
        fields, rows = step(fields, rows)
    spare = EDGE - 2 * STEPS
    return jnp.stack([x[spare:-spare] for x in fields])


def local(replica_variables, analysis, labels, pairing):
    members = lax.axis_size("mem")
    x = replica_variables[0]
    fields, local_rows, width = x.shape
    chunk = width // members
    before, after = edges(x, 1)
    first = flow(before, x, after)

    a_before, a_after = edges(analysis, 1)
    up, down = neighbours("lat")
    coded = labels + 1
    l_before, l_after = edges(coded, 0)
    coded = jnp.concatenate([l_before, coded, l_after], axis=0)
    region = jnp.arange(1, REGIONS + 1, dtype=jnp.int32)
    onehot = (coded[..., None] == region).astype(jnp.float32)
    mid = onehot[EDGE:-EDGE]
    weight = 0.25 * (onehot[EDGE - 1 : -EDGE - 1] + 2.0 * mid + onehot[EDGE + 1 : -EDGE + 1])
    cells = mid.sum((0, 1)) * TILE

    pieces = first.reshape(fields, local_rows, members, chunk).transpose(2, 0, 1, 3)
    everyone = lax.all_to_all(pieces, "mem", 0, 0, tiled=True)
    spread = 0.5 * (everyone - everyone[pairing])
    energy = 0.5 * jnp.sum(spread * spread, axis=1)
    tiles = chunk // TILE
    tile_sums = energy.reshape(members, local_rows, tiles, TILE).sum(-1)
    own_weight = lax.dynamic_slice_in_dim(weight, lax.axis_index("mem") * tiles, tiles, axis=1)
    partial = jnp.einsum("mrt,rtk->mk", tile_sums, own_weight, precision=lax.Precision.HIGHEST)
    sums = jnp.concatenate([partial, cells[None]], axis=0)
    lat_size = lax.axis_size("lat")
    sums = lax.all_to_all(
        jnp.broadcast_to(sums[None], (lat_size,) + sums.shape), "lat", 0, 0, tiled=True
    ).sum(0)
    region_sum = lax.all_to_all(sums[:members], "mem", 0, 0, tiled=True).sum(0)
    factor = target_size / jnp.sqrt(region_sum / sums[members] + small_eps)

    back = lax.all_to_all(spread, "mem", 0, 0, tiled=True)
    b_before, b_after = edges(back, 2)

    def joined(part):
        return part.transpose(1, 2, 0, 3).reshape(fields, part.shape[2], width)

    cell_factor = jnp.einsum("k,rtk->rt", factor, onehot, precision=lax.Precision.HIGHEST)

    def recentred(centre, part, scale):
        scale = jnp.repeat(scale, TILE, axis=1)
        return centre + scale[None] * joined(part)

    closing = flow(
        recentred(a_before, b_before, cell_factor[:EDGE]),
        recentred(analysis, back, cell_factor[EDGE:-EDGE]),
        recentred(a_after, b_after, cell_factor[-EDGE:]),
    )
    return closing[None], factor[None]


def solution(mesh):
    return jax.shard_map(
        local,
        mesh=mesh,
        in_specs=(P("mem", None, "lat", None), P(None, "lat", None), P("lat", None), P()),
        out_specs=(P("mem", None, "lat", None), P("mem", None)),
        check_vma=False,
    )
```

```python
import functools

import jax
import jax.numpy as jnp
from jax import lax
from jax.experimental import pallas as pl
from jax.experimental.pallas import tpu as pltpu
from jax.sharding import PartitionSpec as P

TILE = 128
REGIONS = 8
STEPS = 3
STRIP = 8

grav_coef = 0.1
depth_coef = 0.1
advect_coef = 0.05
diffuse_coef = 0.05
coriolis_coef = 0.05
target_size = 0.5
small_eps = 1e-06

VMEM = pl.BlockSpec(memory_space=pltpu.VMEM)
SMEM = pl.BlockSpec(memory_space=pltpu.SMEM)


def east(field):
    return pltpu.roll(field, field.shape[1] - 1, 1)


def west(field):
    return pltpu.roll(field, 1, 1)


def pack_edges(h, u, v, q, label_row):
    last, first = slice(8, 16), slice(0, 8)
    up = jnp.concatenate(
        [v[last], label_row(15), h[9:16], q[13:16], u[11:16]], axis=0
    )
    down = jnp.concatenate(
        [v[first], h[0:7], label_row(0), u[0:5], q[0:3]], axis=0
    )
    return up, down


def flow_kernel(total_rows, chunks, where_ref, mid_ref, before_ref, after_ref, out_ref, *state):
    hs, us, vs, qs, h1s = state
    lat = where_ref[0]
    last = where_ref[1]
    local_rows = mid_ref.shape[1]
    width = mid_ref.shape[2]
    strips = local_rows // STRIP + 2
    pad = STRIP

    def rows(s, shift=0):
        return pl.ds(pad + STRIP * s + shift, STRIP)

    zero = jnp.zeros((STRIP, width), jnp.float32)
    for ref in (hs, us, vs, qs, h1s):
        ref[0:pad, :] = zero
        ref[pad + STRIP * strips :, :] = zero
    for ref, field in ((hs, 0), (us, 1), (vs, 2), (qs, 3)):
        ref[pad + STRIP : pad + STRIP * (strips - 1), :] = mid_ref[field]
    for s, edge in ((0, before_ref), (strips - 1, after_ref)):
        vs[rows(s), :] = edge[0:8, :]
        hs[rows(s), :] = edge[8:16, :]
        us[rows(s), :] = edge[16:24, :]
    qs[rows(0), :] = pltpu.roll(before_ref[16:24, :], 5, 0)
    qs[rows(strips - 1), :] = pltpu.roll(after_ref[16:24, :], 3, 0)

    inside = [None] * strips
    inside[0] = jnp.where(lat > 0, 1.0, 0.0).astype(jnp.float32)
    inside[-1] = jnp.where(lat < last, 1.0, 0.0).astype(jnp.float32)

    def kept(value, s):
        return value if inside[s] is None else value * inside[s]

    lane_rows = lax.broadcasted_iota(jnp.int32, (STRIP, width), 0)

    def coriolis(s):
        row = (lane_rows + (lat * local_rows + STRIP * (s - 1))).astype(jnp.float32)
        return coriolis_coef * (2.0 * (row + 0.5) / total_rows - 1.0)

    for k in range(STEPS):
        final = k == STEPS - 1
        for s in range(strips):
            u = us[rows(s), :]
            h1s[rows(s), :] = kept(
                hs[rows(s), :]
                - depth_coef
                * ((east(u) - west(u)) + (vs[rows(s, 1), :] - vs[rows(s, -1), :])),
                s,
            )
        carried = qs[rows(0, -1), :]
        for s in range(1, strips - 1) if final else range(strips):
            f = coriolis(s)
            h1 = h1s[rows(s), :]
            v = vs[rows(s), :]
            u1 = us[rows(s), :] + f * v - grav_coef * (east(h1) - west(h1))
            v1 = v - f * u1 - grav_coef * (h1s[rows(s, 1), :] - h1s[rows(s, -1), :])
            q = qs[rows(s), :]
            if final:
                south = qs[rows(s, -1), :]
            else:
                south = carried
                if s < strips - 1:
                    carried = qs[rows(s + 1, -1), :]
            north = qs[rows(s, 1), :]
            e, w = east(q), west(q)
            q1 = (
                q
                - advect_coef * (u1 * (e - w) + v1 * (north - south))
                + diffuse_coef * ((e + w) + (north + south) - 4.0 * q)
            )
            if not final:
                us[rows(s), :] = kept(u1, s)
                vs[rows(s), :] = kept(v1, s)
                qs[rows(s), :] = kept(q1, s)
                hs[rows(s), :] = h1
            else:
                at = slice(STRIP * (s - 1), STRIP * s)
                for field, value in enumerate((h1, u1, v1, q1)):
                    if chunks == 1:
                        out_ref[field, at, :] = value
                    else:
                        size = width // chunks
                        for c in range(chunks):
                            out_ref[c, field, at, :] = value[:, c * size : (c + 1) * size]


def flow(where, middle, before, after, total_rows, chunks, name):
    fields, local_rows, width = middle.shape
    shape = (fields, local_rows, width)
    if chunks > 1:
        shape = (chunks, fields, local_rows, width // chunks)
    state = pltpu.VMEM((local_rows + 4 * STRIP, width), jnp.float32)
    return pl.pallas_call(
        functools.partial(flow_kernel, total_rows, chunks),
        out_shape=jax.ShapeDtypeStruct(shape, jnp.float32),
        in_specs=[SMEM, VMEM, VMEM, VMEM],
        out_specs=VMEM,
        scratch_shapes=[state] * 5,
        compiler_params=pltpu.CompilerParams(vmem_limit_bytes=24 << 20),
        cost_estimate=pl.CostEstimate(
            flops=60 * 10 * STRIP * width, bytes_accessed=1 << 22, transcendentals=0
        ),
        name=name,
    )(where, middle, before, after)


def pair_kernel(pairing_ref, all_ref, spread_ref):
    for m in range(all_ref.shape[0]):
        spread_ref[m] = 0.5 * (all_ref[m] - all_ref[pairing_ref[m]])


def pair_spread(pairing, everyone):
    return pl.pallas_call(
        pair_kernel,
        out_shape=jax.ShapeDtypeStruct(everyone.shape, jnp.float32),
        in_specs=[SMEM, VMEM],
        out_specs=VMEM,
        compiler_params=pltpu.CompilerParams(vmem_limit_bytes=8 << 20),
        cost_estimate=pl.CostEstimate(flops=1 << 19, bytes_accessed=3 << 20, transcendentals=0),
        name="pair_spread",
    )(pairing, everyone)


def region_kernel(spread_ref, labels_ref, out_ref):
    members = spread_ref.shape[0]
    local_rows = spread_ref.shape[2]
    lane = lax.broadcasted_iota(jnp.int32, (REGIONS, TILE), 1)

    def folded(x):
        x = x[:STRIP] + x[STRIP:]
        return x[:, :TILE] + x[:, TILE:]

    here = labels_ref[1]
    weights, counts = [], []
    for r in range(REGIONS):
        code = float(r + 1)

        def is_r(x):
            return jnp.where(x == code, 1.0, 0.0).astype(jnp.float32)

        own = is_r(here)
        counts.append(jnp.sum(folded(own), axis=0, keepdims=True))
        weights.append(0.125 * (is_r(labels_ref[0]) + 2.0 * own + is_r(labels_ref[2])))

    def placed(rows, at, total):
        column = jnp.sum(jnp.concatenate(rows, axis=0), axis=1, keepdims=True)
        return jnp.where(lane == at, column, total)

    total = placed(counts, members, jnp.zeros((REGIONS, TILE), jnp.float32))
    for m in range(members):
        square = None
        for field in range(spread_ref.shape[1]):
            x = spread_ref[m, field]
            square = x * x if square is None else square + x * x
        total = placed(
            [jnp.sum(folded(square * w), axis=0, keepdims=True) for w in weights], m, total
        )
    out_ref[...] = total


def region_share(spread, labels):
    return pl.pallas_call(
        region_kernel,
        out_shape=jax.ShapeDtypeStruct((REGIONS, TILE), jnp.float32),
        in_specs=[VMEM, VMEM],
        out_specs=VMEM,
        compiler_params=pltpu.CompilerParams(vmem_limit_bytes=8 << 20),
        cost_estimate=pl.CostEstimate(flops=1 << 20, bytes_accessed=1 << 20, transcendentals=0),
        name="region_share",
    )(spread, labels)


def recentre_kernel(factor_ref, labels_ref, analysis_ref, back_ref, mid_ref, up_ref, down_ref):
    chunks, fields, local_rows, size = back_ref.shape
    labels = labels_ref[...]
    factor = factor_ref[...]
    scale = jnp.zeros(labels.shape, jnp.float32)
    for r in range(REGIONS):
        scale = jnp.where(labels == float(r + 1), factor[r : r + 1, :], scale)
    for c in range(chunks):
        at = slice(c * size, (c + 1) * size)
        wide = jnp.concatenate(
            [
                jnp.broadcast_to(scale[:, t : t + 1], (local_rows, TILE))
                for t in range(c * size // TILE, (c + 1) * size // TILE)
            ],
            axis=1,
        )
        h, u, v, q = [analysis_ref[i, :, at] + wide * back_ref[c, i] for i in range(fields)]
        for i, value in enumerate((h, u, v, q)):
            mid_ref[i, :, at] = value
        row = lax.broadcasted_iota(jnp.int32, (STRIP, size), 0)
        up_ref[0:8, at] = v[8:16]
        up_ref[8:16, at] = h[8:16]
        up_ref[16:24, at] = jnp.where(row < 3, pltpu.roll(q[8:16], 3, 0), u[8:16])
        down_ref[0:8, at] = v[0:8]
        down_ref[8:16, at] = h[0:8]
        down_ref[16:24, at] = jnp.where(row >= 5, pltpu.roll(q[0:8], 5, 0), u[0:8])


def recentre(factor, labels, analysis, back):
    fields, local_rows, width = analysis.shape
    edge = jax.ShapeDtypeStruct((3 * STRIP, width), jnp.float32)
    return pl.pallas_call(
        recentre_kernel,
        out_shape=(jax.ShapeDtypeStruct(analysis.shape, jnp.float32), edge, edge),
        in_specs=[VMEM] * 4,
        out_specs=(VMEM,) * 3,
        compiler_params=pltpu.CompilerParams(vmem_limit_bytes=12 << 20),
        cost_estimate=pl.CostEstimate(flops=1 << 20, bytes_accessed=4 << 20, transcendentals=0),
        name="recentre",
    )(factor, labels, analysis, back)


def all_sum(value):
    for axis in ("lat", "mem"):
        size = lax.axis_size(axis)
        for stride in (1, 4):
            others = [
                lax.ppermute(value, axis, [(i, i ^ (d * stride)) for i in range(size)])
                for d in (1, 2, 3)
            ]
            value = (value + others[0]) + (others[1] + others[2])
    return value


def local(replica_variables, analysis, labels, pairing):
    members = lax.axis_size("mem")
    lat_size = lax.axis_size("lat")
    lat = lax.axis_index("lat")
    member = lax.axis_index("mem")
    x = replica_variables[0]
    fields, local_rows, width = x.shape
    chunk = width // members
    tiles = chunk // TILE
    total_rows = float(local_rows * lat_size)
    where = jnp.stack([lat, jnp.int32(lat_size - 1)]).astype(jnp.int32)
    up = [(i, i + 1) for i in range(lat_size - 1)]
    down = [(j, i) for i, j in up]

    coded = (labels + 1).astype(jnp.float32)
    wide = jnp.pad(coded, ((0, 0), (0, width - coded.shape[1])))
    last, first = pack_edges(x[0], x[1], x[2], x[3], lambda i: wide[i : i + 1])
    before = lax.ppermute(last, "lat", up)
    after = lax.ppermute(first, "lat", down)
    pieces = flow(where, x, before, after, total_rows, members, "first_flow")
    everyone = lax.all_to_all(pieces, "mem", 0, 0, tiled=True)

    tile_count = coded.shape[1]
    rows = jnp.concatenate([before[8:9, :tile_count], coded, after[15:16, :tile_count]], axis=0)
    own = lax.dynamic_slice_in_dim(rows, member * tiles, tiles, axis=1)
    own = jnp.repeat(own, TILE, axis=1)
    own = jnp.stack([own[:-2], own[1:-1], own[2:]])

    spread = pair_spread(pairing, everyone)
    back = lax.all_to_all(spread, "mem", 0, 0, tiled=True)
    sums = all_sum(region_share(spread, own))
    region_sum = lax.dynamic_slice_in_dim(sums, member, 1, axis=1)
    cells = sums[:, members : members + 1]
    factor = target_size / jnp.sqrt(region_sum / cells + small_eps)

    lane_labels = jnp.pad(coded, ((0, 0), (0, TILE - tile_count)))
    middle, last, first = recentre(
        jnp.broadcast_to(factor, (REGIONS, TILE)), lane_labels, analysis, back
    )
    before = lax.ppermute(last, "lat", up)
    after = lax.ppermute(first, "lat", down)
    closing = flow(where, middle, before, after, total_rows, 1, "closing_flow")
    return closing[None], factor.reshape(1, REGIONS)


def solution(mesh):
    return jax.shard_map(
        local,
        mesh=mesh,
        in_specs=(P("mem", None, "lat", None), P(None, "lat", None), P("lat", None), P()),
        out_specs=(P("mem", None, "lat", None), P("mem", None)),
        check_vma=False,
    )
```

```python
import functools

import jax
import jax.numpy as jnp
from jax import lax
from jax.experimental import pallas as pl
from jax.experimental.pallas import tpu as pltpu
from jax.sharding import PartitionSpec as P

TILE = 128
REGIONS = 8
STEPS = 3
STRIP = 8

grav_coef = 0.1
depth_coef = 0.1
advect_coef = 0.05
diffuse_coef = 0.05
coriolis_coef = 0.05
target_size = 0.5
small_eps = 1e-06

VMEM = pl.BlockSpec(memory_space=pltpu.VMEM)
SMEM = pl.BlockSpec(memory_space=pltpu.SMEM)


def east(field):
    return pltpu.roll(field, field.shape[1] - 1, 1)


def west(field):
    return pltpu.roll(field, 1, 1)


def pack_rows(up_ref, down_ref, at, h, u, v, q):
    row = lax.broadcasted_iota(jnp.int32, (STRIP, v.shape[1]), 0)
    up_ref[0:8, at] = v[8:16]
    up_ref[8:16, at] = h[8:16]
    up_ref[16:24, at] = jnp.where(row < 3, pltpu.roll(q[8:16], 3, 0), u[8:16])
    down_ref[0:8, at] = v[0:8]
    down_ref[8:16, at] = h[0:8]
    down_ref[16:24, at] = jnp.where(row >= 5, pltpu.roll(q[0:8], 5, 0), u[0:8])


def edge_kernel(fields_ref, labels_ref, up_ref, down_ref):
    width = fields_ref.shape[2]
    size = width // 8
    for c in range(8):
        at = slice(c * size, (c + 1) * size)
        h, u, v, q = [fields_ref[i, :, at] for i in range(4)]
        pack_rows(up_ref, down_ref, at, h, u, v, q)
    up_ref[8:9, 0:TILE] = labels_ref[15:16, :]
    down_ref[15:16, 0:TILE] = labels_ref[0:1, :]


def packed_edges(fields, labels):
    edge = jax.ShapeDtypeStruct((3 * STRIP, fields.shape[2]), jnp.float32)
    return pl.pallas_call(
        edge_kernel,
        out_shape=(edge, edge),
        in_specs=[VMEM, VMEM],
        out_specs=(VMEM, VMEM),
        compiler_params=pltpu.CompilerParams(vmem_limit_bytes=8 << 20),
        cost_estimate=pl.CostEstimate(flops=1 << 18, bytes_accessed=2 << 20, transcendentals=0),
        name="packed_edges",
    )(fields, labels)


def flow_kernel(total_rows, chunks, where_ref, mid_ref, before_ref, after_ref, out_ref, *state):
    hs, us, vs, qs, h1s = state
    lat = where_ref[0]
    last = where_ref[1]
    local_rows = mid_ref.shape[1]
    width = mid_ref.shape[2]
    strips = local_rows // STRIP + 2
    pad = STRIP

    def rows(s, shift=0):
        return pl.ds(pad + STRIP * s + shift, STRIP)

    zero = jnp.zeros((STRIP, width), jnp.float32)
    for ref in (hs, us, vs, qs, h1s):
        ref[0:pad, :] = zero
        ref[pad + STRIP * strips :, :] = zero
    for ref, field in ((hs, 0), (us, 1), (vs, 2), (qs, 3)):
        ref[pad + STRIP : pad + STRIP * (strips - 1), :] = mid_ref[field]
    for s, edge in ((0, before_ref), (strips - 1, after_ref)):
        vs[rows(s), :] = edge[0:8, :]
        hs[rows(s), :] = edge[8:16, :]
        us[rows(s), :] = edge[16:24, :]
    qs[rows(0), :] = pltpu.roll(before_ref[16:24, :], 5, 0)
    qs[rows(strips - 1), :] = pltpu.roll(after_ref[16:24, :], 3, 0)

    inside = [None] * strips
    inside[0] = jnp.where(lat > 0, 1.0, 0.0).astype(jnp.float32)
    inside[-1] = jnp.where(lat < last, 1.0, 0.0).astype(jnp.float32)

    def kept(value, s):
        return value if inside[s] is None else value * inside[s]

    lane_rows = lax.broadcasted_iota(jnp.int32, (STRIP, width), 0)

    def coriolis(s):
        row = (lane_rows + (lat * local_rows + STRIP * (s - 1))).astype(jnp.float32)
        return coriolis_coef * (2.0 * (row + 0.5) / total_rows - 1.0)

    for k in range(STEPS):
        final = k == STEPS - 1
        for s in range(strips):
            u = us[rows(s), :]
            h1s[rows(s), :] = kept(
                hs[rows(s), :]
                - depth_coef
                * ((east(u) - west(u)) + (vs[rows(s, 1), :] - vs[rows(s, -1), :])),
                s,
            )
        carried = qs[rows(0, -1), :]
        for s in range(1, strips - 1) if final else range(strips):
            f = coriolis(s)
            h1 = h1s[rows(s), :]
            v = vs[rows(s), :]
            u1 = us[rows(s), :] + f * v - grav_coef * (east(h1) - west(h1))
            v1 = v - f * u1 - grav_coef * (h1s[rows(s, 1), :] - h1s[rows(s, -1), :])
            q = qs[rows(s), :]
            if final:
                south = qs[rows(s, -1), :]
            else:
                south = carried
                if s < strips - 1:
                    carried = qs[rows(s + 1, -1), :]
            north = qs[rows(s, 1), :]
            e, w = east(q), west(q)
            q1 = (
                q
                - advect_coef * (u1 * (e - w) + v1 * (north - south))
                + diffuse_coef * ((e + w) + (north + south) - 4.0 * q)
            )
            if not final:
                us[rows(s), :] = kept(u1, s)
                vs[rows(s), :] = kept(v1, s)
                qs[rows(s), :] = kept(q1, s)
                hs[rows(s), :] = h1
            else:
                at = slice(STRIP * (s - 1), STRIP * s)
                for field, value in enumerate((h1, u1, v1, q1)):
                    if chunks == 1:
                        out_ref[field, at, :] = value
                    else:
                        size = width // chunks
                        for c in range(chunks):
                            out_ref[c, field, at, :] = value[:, c * size : (c + 1) * size]


def flow(where, middle, before, after, total_rows, chunks, name):
    fields, local_rows, width = middle.shape
    shape = (fields, local_rows, width)
    if chunks > 1:
        shape = (chunks, fields, local_rows, width // chunks)
    state = pltpu.VMEM((local_rows + 4 * STRIP, width), jnp.float32)
    return pl.pallas_call(
        functools.partial(flow_kernel, total_rows, chunks),
        out_shape=jax.ShapeDtypeStruct(shape, jnp.float32),
        in_specs=[SMEM, VMEM, VMEM, VMEM],
        out_specs=VMEM,
        scratch_shapes=[state] * 5,
        compiler_params=pltpu.CompilerParams(vmem_limit_bytes=24 << 20),
        cost_estimate=pl.CostEstimate(
            flops=60 * 10 * STRIP * width, bytes_accessed=1 << 22, transcendentals=0
        ),
        name=name,
    )(where, middle, before, after)


def pair_kernel(pairing_ref, all_ref, labels_ref, spread_ref, share_ref):
    members, fields, local_rows, size = all_ref.shape
    tiles = size // TILE
    lane = lax.broadcasted_iota(jnp.int32, (REGIONS, TILE), 1)

    def folded(x):
        return x[:STRIP] + x[STRIP:]

    weights, counts = [], []
    shown = [
        [
            jnp.broadcast_to(labels_ref[i : i + local_rows, t : t + 1], (local_rows, TILE))
            for t in range(tiles)
        ]
        for i in range(3)
    ]
    for r in range(REGIONS):

        def is_r(x):
            return jnp.where(x == float(r + 1), 1.0, 0.0).astype(jnp.float32)

        count, weight = None, []
        for t in range(tiles):
            own = is_r(shown[1][t])
            count = folded(own) if count is None else count + folded(own)
            weight.append(0.125 * (is_r(shown[0][t]) + 2.0 * own + is_r(shown[2][t])))
        counts.append(jnp.sum(count, axis=0, keepdims=True))
        weights.append(weight)

    def placed(rows, at, total):
        column = jnp.sum(jnp.concatenate(rows, axis=0), axis=1, keepdims=True)
        return jnp.where(lane == at, column, total)

    total = placed(counts, members, jnp.zeros((REGIONS, TILE), jnp.float32))
    for m in range(members):
        partner = pairing_ref[m]
        squares = [None] * tiles
        for field in range(fields):
            spread = 0.5 * (all_ref[m, field] - all_ref[partner, field])
            for t in range(tiles):
                x = spread[:, t * TILE : (t + 1) * TILE]
                at = (field * tiles + t) * local_rows
                spread_ref[m, at : at + local_rows, :] = x
                squares[t] = x * x if squares[t] is None else squares[t] + x * x
        spread_ref[m, fields * tiles * local_rows :, :] = jnp.zeros((REGIONS, TILE), jnp.float32)
        parts = []
        for weight in weights:
            part = None
            for t in range(tiles):
                y = folded(squares[t] * weight[t])
                part = y if part is None else part + y
            parts.append(jnp.sum(part, axis=0, keepdims=True))
        total = placed(parts, m, total)
    share_ref[...] = total


def pair_spread(pairing, everyone, labels):
    members, fields, local_rows, size = everyone.shape
    rows = fields * local_rows * size // TILE + REGIONS
    return pl.pallas_call(
        pair_kernel,
        out_shape=(
            jax.ShapeDtypeStruct((members, rows, TILE), jnp.float32),
            jax.ShapeDtypeStruct((REGIONS, TILE), jnp.float32),
        ),
        in_specs=[SMEM, VMEM, VMEM],
        out_specs=(VMEM, VMEM),
        compiler_params=pltpu.CompilerParams(vmem_limit_bytes=8 << 20),
        cost_estimate=pl.CostEstimate(flops=1 << 20, bytes_accessed=3 << 20, transcendentals=0),
        name="pair_spread",
    )(pairing, everyone, labels)


def recentre_kernel(
    labels_ref, analysis_ref, back_ref, mid_ref, up_ref, down_ref, factor_ref
):
    chunks = back_ref.shape[0]
    fields, local_rows, width = analysis_ref.shape
    tiles = width // chunks // TILE
    tail = fields * tiles * local_rows
    sums = back_ref[0, tail:, :]
    for c in range(1, chunks):
        sums = sums + back_ref[c, tail:, :]
    region_sum = jnp.broadcast_to(sums[:, 0:1], (REGIONS, TILE))
    cells = jnp.broadcast_to(sums[:, 1:2], (REGIONS, TILE))
    factor = target_size / jnp.sqrt(region_sum / cells + small_eps)
    factor_ref[...] = factor
    labels = labels_ref[...]
    scale = jnp.zeros(labels.shape, jnp.float32)
    for r in range(REGIONS):
        scale = jnp.where(labels == float(r + 1), factor[r : r + 1, :], scale)
    for c in range(chunks):
        for t in range(tiles):
            tile = c * tiles + t
            at = slice(tile * TILE, (tile + 1) * TILE)
            wide = jnp.broadcast_to(scale[:, tile : tile + 1], (local_rows, TILE))
            values = []
            for i in range(fields):
                row = (i * tiles + t) * local_rows
                value = analysis_ref[i, :, at] + wide * back_ref[c, row : row + local_rows, :]
                mid_ref[i, :, at] = value
                values.append(value)
            pack_rows(up_ref, down_ref, at, *values)


def recentre(labels, analysis, back):
    edge = jax.ShapeDtypeStruct((3 * STRIP, analysis.shape[2]), jnp.float32)
    return pl.pallas_call(
        recentre_kernel,
        out_shape=(
            jax.ShapeDtypeStruct(analysis.shape, jnp.float32),
            edge,
            edge,
            jax.ShapeDtypeStruct((REGIONS, TILE), jnp.float32),
        ),
        in_specs=[VMEM] * 3,
        out_specs=(VMEM,) * 4,
        compiler_params=pltpu.CompilerParams(vmem_limit_bytes=12 << 20),
        cost_estimate=pl.CostEstimate(flops=1 << 20, bytes_accessed=4 << 20, transcendentals=0),
        name="recentre",
    )(labels, analysis, back)


def local(replica_variables, analysis, labels, pairing):
    members = lax.axis_size("mem")
    lat_size = lax.axis_size("lat")
    lat = lax.axis_index("lat")
    member = lax.axis_index("mem")
    x = replica_variables[0]
    fields, local_rows, width = x.shape
    tiles = width // members // TILE
    total_rows = float(local_rows * lat_size)
    where = jnp.stack([lat, jnp.int32(lat_size - 1)]).astype(jnp.int32)
    up = [(i, i + 1) for i in range(lat_size - 1)]
    down = [(j, i) for i, j in up]

    coded = (labels + 1).astype(jnp.float32)
    coded = jnp.pad(coded, ((0, 0), (0, TILE - labels.shape[1])))
    last, first = packed_edges(x, coded)
    before = lax.ppermute(last, "lat", up)
    after = lax.ppermute(first, "lat", down)
    pieces = flow(where, x, before, after, total_rows, members, "first_flow")
    everyone = lax.all_to_all(pieces, "mem", 0, 0, tiled=True)

    rows = jnp.concatenate([before[8:9, :TILE], coded, after[15:16, :TILE]], axis=0)
    own = lax.dynamic_slice_in_dim(rows, member * tiles, tiles, axis=1)
    own = jnp.pad(own, ((0, 6), (0, TILE - tiles)))
    spread, share = pair_spread(pairing, everyone, own)
    share = lax.all_to_all(
        jnp.broadcast_to(share[None], (lat_size,) + share.shape), "lat", 0, 0, tiled=True
    ).sum(0)
    lane = jnp.arange(TILE)
    tail = jnp.where(
        lane == 0,
        share.T[:members, :, None],
        jnp.where(lane == 1, share[None, :, members : members + 1], 0.0),
    )
    spread = lax.dynamic_update_slice(spread, tail, (0, spread.shape[1] - REGIONS, 0))
    back = lax.all_to_all(spread, "mem", 0, 0, tiled=True)

    middle, last, first, factor = recentre(coded, analysis, back)
    before = lax.ppermute(last, "lat", up)
    after = lax.ppermute(first, "lat", down)
    closing = flow(where, middle, before, after, total_rows, 1, "closing_flow")
    return closing[None], factor[:, 0].reshape(1, REGIONS)


def solution(mesh):
    return jax.shard_map(
        local,
        mesh=mesh,
        in_specs=(P("mem", None, "lat", None), P(None, "lat", None), P("lat", None), P()),
        out_specs=(P("mem", None, "lat", None), P("mem", None)),
        check_vma=False,
    )
```

```python
import functools

import jax
import jax.numpy as jnp
from jax import lax
from jax.experimental import pallas as pl
from jax.experimental.pallas import tpu as pltpu
from jax.sharding import PartitionSpec as P

TILE = 128
REGIONS = 8
STEPS = 3
STRIP = 8

grav_coef = 0.1
depth_coef = 0.1
advect_coef = 0.05
diffuse_coef = 0.05
coriolis_coef = 0.05
target_size = 0.5
small_eps = 1e-06

VMEM = pl.BlockSpec(memory_space=pltpu.VMEM)
SMEM = pl.BlockSpec(memory_space=pltpu.SMEM)


def east(field):
    return pltpu.roll(field, field.shape[1] - 1, 1)


def west(field):
    return pltpu.roll(field, 1, 1)


def pack_rows(up_ref, down_ref, at, h, u, v, q):
    row = lax.broadcasted_iota(jnp.int32, (STRIP, v.shape[1]), 0)
    up_ref[0:8, at] = v[8:16]
    up_ref[8:16, at] = h[8:16]
    up_ref[16:24, at] = jnp.where(row < 3, pltpu.roll(q[8:16], 3, 0), u[8:16])
    down_ref[0:8, at] = v[0:8]
    down_ref[8:16, at] = h[0:8]
    down_ref[16:24, at] = jnp.where(row >= 5, pltpu.roll(q[0:8], 5, 0), u[0:8])


def edge_kernel(fields_ref, labels_ref, up_ref, down_ref):
    width = fields_ref.shape[2]
    size = width // 8
    for c in range(8):
        at = slice(c * size, (c + 1) * size)
        h, u, v, q = [fields_ref[i, :, at] for i in range(4)]
        pack_rows(up_ref, down_ref, at, h, u, v, q)
    up_ref[8:9, 0:TILE] = labels_ref[15:16, :]
    down_ref[15:16, 0:TILE] = labels_ref[0:1, :]


def packed_edges(fields, labels):
    edge = jax.ShapeDtypeStruct((3 * STRIP, fields.shape[2]), jnp.float32)
    return pl.pallas_call(
        edge_kernel,
        out_shape=(edge, edge),
        in_specs=[VMEM, VMEM],
        out_specs=(VMEM, VMEM),
        compiler_params=pltpu.CompilerParams(vmem_limit_bytes=8 << 20),
        cost_estimate=pl.CostEstimate(flops=1 << 18, bytes_accessed=2 << 20, transcendentals=0),
        name="packed_edges",
    )(fields, labels)


def flow_kernel(total_rows, chunks, where_ref, mid_ref, before_ref, after_ref, out_ref, *state):
    hs, us, vs, qs, h1s = state
    lat = where_ref[0]
    last = where_ref[1]
    local_rows = mid_ref.shape[1]
    width = mid_ref.shape[2]
    strips = local_rows // STRIP + 2
    pad = STRIP

    def rows(s, shift=0):
        return pl.ds(pad + STRIP * s + shift, STRIP)

    zero = jnp.zeros((STRIP, width), jnp.float32)
    for ref in (hs, us, vs, qs, h1s):
        ref[0:pad, :] = zero
        ref[pad + STRIP * strips :, :] = zero
    for ref, field in ((hs, 0), (us, 1), (vs, 2), (qs, 3)):
        ref[pad + STRIP : pad + STRIP * (strips - 1), :] = mid_ref[field]
    for s, edge in ((0, before_ref), (strips - 1, after_ref)):
        vs[rows(s), :] = edge[0:8, :]
        hs[rows(s), :] = edge[8:16, :]
        us[rows(s), :] = edge[16:24, :]
    qs[rows(0), :] = pltpu.roll(before_ref[16:24, :], 5, 0)
    qs[rows(strips - 1), :] = pltpu.roll(after_ref[16:24, :], 3, 0)

    inside = [None] * strips
    inside[0] = jnp.where(lat > 0, 1.0, 0.0).astype(jnp.float32)
    inside[-1] = jnp.where(lat < last, 1.0, 0.0).astype(jnp.float32)

    def kept(value, s):
        return value if inside[s] is None else value * inside[s]

    lane_rows = lax.broadcasted_iota(jnp.int32, (STRIP, width), 0)

    def coriolis(s):
        row = (lane_rows + (lat * local_rows + STRIP * (s - 1))).astype(jnp.float32)
        return coriolis_coef * (2.0 * (row + 0.5) / total_rows - 1.0)

    for k in range(STEPS):
        final = k == STEPS - 1
        for s in range(strips):
            u = us[rows(s), :]
            h1s[rows(s), :] = kept(
                hs[rows(s), :]
                - depth_coef
                * ((east(u) - west(u)) + (vs[rows(s, 1), :] - vs[rows(s, -1), :])),
                s,
            )
        carried = qs[rows(0, -1), :]
        for s in range(1, strips - 1) if final else range(strips):
            f = coriolis(s)
            h1 = h1s[rows(s), :]
            v = vs[rows(s), :]
            u1 = us[rows(s), :] + f * v - grav_coef * (east(h1) - west(h1))
            v1 = v - f * u1 - grav_coef * (h1s[rows(s, 1), :] - h1s[rows(s, -1), :])
            q = qs[rows(s), :]
            if final:
                south = qs[rows(s, -1), :]
            else:
                south = carried
                if s < strips - 1:
                    carried = qs[rows(s + 1, -1), :]
            north = qs[rows(s, 1), :]
            e, w = east(q), west(q)
            q1 = (
                q
                - advect_coef * (u1 * (e - w) + v1 * (north - south))
                + diffuse_coef * ((e + w) + (north + south) - 4.0 * q)
            )
            if not final:
                us[rows(s), :] = kept(u1, s)
                vs[rows(s), :] = kept(v1, s)
                qs[rows(s), :] = kept(q1, s)
                hs[rows(s), :] = h1
            else:
                at = slice(STRIP * (s - 1), STRIP * s)
                for field, value in enumerate((h1, u1, v1, q1)):
                    if chunks == 1:
                        out_ref[field, at, :] = value
                    else:
                        size = width // chunks
                        for c in range(chunks):
                            out_ref[c, field, at, :] = value[:, c * size : (c + 1) * size]


def flow(where, middle, before, after, total_rows, chunks, name):
    fields, local_rows, width = middle.shape
    shape = (fields, local_rows, width)
    if chunks > 1:
        shape = (chunks, fields, local_rows, width // chunks)
    state = pltpu.VMEM((local_rows + 4 * STRIP, width), jnp.float32)
    return pl.pallas_call(
        functools.partial(flow_kernel, total_rows, chunks),
        out_shape=jax.ShapeDtypeStruct(shape, jnp.float32),
        in_specs=[SMEM, VMEM, VMEM, VMEM],
        out_specs=VMEM,
        scratch_shapes=[state] * 5,
        compiler_params=pltpu.CompilerParams(vmem_limit_bytes=24 << 20),
        cost_estimate=pl.CostEstimate(
            flops=60 * 10 * STRIP * width, bytes_accessed=1 << 22, transcendentals=0
        ),
        name=name,
    )(where, middle, before, after)


def pair_kernel(pairing_ref, all_ref, labels_ref, spread_ref):
    members, fields, local_rows, size = all_ref.shape
    tiles = size // TILE
    lane = lax.broadcasted_iota(jnp.int32, (REGIONS, TILE), 1)

    def folded(x):
        return x[:STRIP] + x[STRIP:]

    weights, counts = [], []
    shown = [
        [
            jnp.broadcast_to(labels_ref[i : i + local_rows, t : t + 1], (local_rows, TILE))
            for t in range(tiles)
        ]
        for i in range(3)
    ]
    for r in range(REGIONS):

        def is_r(x):
            return jnp.where(x == float(r + 1), 1.0, 0.0).astype(jnp.float32)

        count, weight = None, []
        for t in range(tiles):
            own = is_r(shown[1][t])
            count = folded(own) if count is None else count + folded(own)
            weight.append(0.125 * (is_r(shown[0][t]) + 2.0 * own + is_r(shown[2][t])))
        counts.append(jnp.sum(count, axis=0, keepdims=True))
        weights.append(weight)

    def column(rows):
        return jnp.sum(jnp.concatenate(rows, axis=0), axis=1, keepdims=True)

    empty = jnp.where(lane == 1, column(counts), 0.0)
    for m in range(members):
        partner = pairing_ref[m]
        squares = [None] * tiles
        for field in range(fields):
            spread = 0.5 * (all_ref[m, field] - all_ref[partner, field])
            for t in range(tiles):
                x = spread[:, t * TILE : (t + 1) * TILE]
                at = (field * tiles + t) * local_rows
                spread_ref[m, at : at + local_rows, :] = x
                squares[t] = x * x if squares[t] is None else squares[t] + x * x
        parts = []
        for weight in weights:
            part = None
            for t in range(tiles):
                y = folded(squares[t] * weight[t])
                part = y if part is None else part + y
            parts.append(jnp.sum(part, axis=0, keepdims=True))
        spread_ref[m, fields * tiles * local_rows :, :] = jnp.where(
            lane == 0, column(parts), empty
        )


def pair_spread(pairing, everyone, labels):
    members, fields, local_rows, size = everyone.shape
    rows = fields * local_rows * size // TILE + REGIONS
    return pl.pallas_call(
        pair_kernel,
        out_shape=jax.ShapeDtypeStruct((members, rows, TILE), jnp.float32),
        in_specs=[SMEM, VMEM, VMEM],
        out_specs=VMEM,
        compiler_params=pltpu.CompilerParams(vmem_limit_bytes=8 << 20),
        cost_estimate=pl.CostEstimate(flops=1 << 20, bytes_accessed=3 << 20, transcendentals=0),
        name="pair_spread",
    )(pairing, everyone, labels)


def recentre_kernel(
    labels_ref, analysis_ref, back_ref, shares_ref, mid_ref, up_ref, down_ref, factor_ref
):
    chunks = back_ref.shape[0]
    fields, local_rows, width = analysis_ref.shape
    tiles = width // chunks // TILE
    sums = jnp.sum(shares_ref[...], axis=0)
    region_sum = jnp.broadcast_to(sums[:, 0:1], (REGIONS, TILE))
    cells = jnp.broadcast_to(sums[:, 1:2], (REGIONS, TILE))
    factor = target_size / jnp.sqrt(region_sum / cells + small_eps)
    factor_ref[...] = factor
    labels = labels_ref[...]
    scale = jnp.zeros(labels.shape, jnp.float32)
    for r in range(REGIONS):
        scale = jnp.where(labels == float(r + 1), factor[r : r + 1, :], scale)
    for c in range(chunks):
        for t in range(tiles):
            tile = c * tiles + t
            at = slice(tile * TILE, (tile + 1) * TILE)
            wide = jnp.broadcast_to(scale[:, tile : tile + 1], (local_rows, TILE))
            values = []
            for i in range(fields):
                row = (i * tiles + t) * local_rows
                value = analysis_ref[i, :, at] + wide * back_ref[c, row : row + local_rows, :]
                mid_ref[i, :, at] = value
                values.append(value)
            pack_rows(up_ref, down_ref, at, *values)


def recentre(labels, analysis, back, shares):
    edge = jax.ShapeDtypeStruct((3 * STRIP, analysis.shape[2]), jnp.float32)
    return pl.pallas_call(
        recentre_kernel,
        out_shape=(
            jax.ShapeDtypeStruct(analysis.shape, jnp.float32),
            edge,
            edge,
            jax.ShapeDtypeStruct((REGIONS, TILE), jnp.float32),
        ),
        in_specs=[VMEM] * 4,
        out_specs=(VMEM,) * 4,
        compiler_params=pltpu.CompilerParams(vmem_limit_bytes=12 << 20),
        cost_estimate=pl.CostEstimate(flops=1 << 20, bytes_accessed=4 << 20, transcendentals=0),
        name="recentre",
    )(labels, analysis, back, shares)


def local(replica_variables, analysis, labels, pairing):
    members = lax.axis_size("mem")
    lat_size = lax.axis_size("lat")
    lat = lax.axis_index("lat")
    member = lax.axis_index("mem")
    x = replica_variables[0]
    fields, local_rows, width = x.shape
    tiles = width // members // TILE
    total_rows = float(local_rows * lat_size)
    where = jnp.stack([lat, jnp.int32(lat_size - 1)]).astype(jnp.int32)
    up = [(i, i + 1) for i in range(lat_size - 1)]
    down = [(j, i) for i, j in up]

    coded = (labels + 1).astype(jnp.float32)
    coded = jnp.pad(coded, ((0, 0), (0, TILE - labels.shape[1])))
    last, first = packed_edges(x, coded)
    before = lax.ppermute(last, "lat", up)
    after = lax.ppermute(first, "lat", down)
    pieces = flow(where, x, before, after, total_rows, members, "first_flow")
    everyone = lax.all_to_all(pieces, "mem", 0, 0, tiled=True)

    rows = jnp.concatenate([before[8:9, :TILE], coded, after[15:16, :TILE]], axis=0)
    own = lax.dynamic_slice_in_dim(rows, member * tiles, tiles, axis=1)
    own = jnp.pad(own, ((0, 6), (0, TILE - tiles)))
    spread = pair_spread(pairing, everyone, own)
    back = lax.all_to_all(spread, "mem", 0, 0, tiled=True)
    share = back[:, back.shape[1] - REGIONS :, :].sum(0)
    shares = lax.all_to_all(
        jnp.broadcast_to(share[None], (lat_size,) + share.shape), "lat", 0, 0, tiled=True
    )
    middle, last, first, factor = recentre(coded, analysis, back, shares)
    before = lax.ppermute(last, "lat", up)
    after = lax.ppermute(first, "lat", down)
    closing = flow(where, middle, before, after, total_rows, 1, "closing_flow")
    return closing[None], factor[:, 0].reshape(1, REGIONS)


def solution(mesh):
    return jax.shard_map(
        local,
        mesh=mesh,
        in_specs=(P("mem", None, "lat", None), P(None, "lat", None), P("lat", None), P()),
        out_specs=(P("mem", None, "lat", None), P("mem", None)),
        check_vma=False,
    )
```

```python
import functools

import jax
import jax.numpy as jnp
from jax import lax
from jax.experimental import pallas as pl
from jax.experimental.pallas import tpu as pltpu
from jax.sharding import PartitionSpec as P

TILE = 128
REGIONS = 8
STEPS = 3
STRIP = 8

grav_coef = 0.1
depth_coef = 0.1
advect_coef = 0.05
diffuse_coef = 0.05
coriolis_coef = 0.05
target_size = 0.5
small_eps = 1e-06

VMEM = pl.BlockSpec(memory_space=pltpu.VMEM)
SMEM = pl.BlockSpec(memory_space=pltpu.SMEM)


def east(field):
    return pltpu.roll(field, field.shape[1] - 1, 1)


def west(field):
    return pltpu.roll(field, 1, 1)


def pack_rows(up_ref, down_ref, at, h, u, v, q):
    row = lax.broadcasted_iota(jnp.int32, (STRIP, v.shape[1]), 0)
    up_ref[0:8, at] = v[8:16]
    up_ref[8:16, at] = h[8:16]
    up_ref[16:24, at] = jnp.where(row < 3, pltpu.roll(q[8:16], 3, 0), u[8:16])
    down_ref[0:8, at] = v[0:8]
    down_ref[8:16, at] = h[0:8]
    down_ref[16:24, at] = jnp.where(row >= 5, pltpu.roll(q[0:8], 5, 0), u[0:8])


def edge_kernel(label_rows, fields_ref, labels_ref, after_ref, up_ref, down_ref):
    width = fields_ref.shape[2]
    size = width // 8
    for c in range(8):
        at = slice(c * size, (c + 1) * size)
        h, u, v, q = [fields_ref[i, :, at] for i in range(4)]
        pack_rows(up_ref, down_ref, at, h, u, v, q)
    for k in range(label_rows):
        at = slice(k * TILE, (k + 1) * TILE)
        row = labels_ref.shape[0] - label_rows + k
        up_ref[8:9, at] = labels_ref[row : row + 1, :]
        down_ref[15:16, at] = labels_ref[k : k + 1, :]


def packed_edges(fields, labels, after, label_rows, name):
    edge = jax.ShapeDtypeStruct((3 * STRIP, fields.shape[2]), jnp.float32)
    return pl.pallas_call(
        functools.partial(edge_kernel, label_rows),
        out_shape=(edge, edge),
        in_specs=[VMEM, VMEM, pl.BlockSpec(memory_space=pl.ANY)],
        out_specs=(VMEM, VMEM),
        compiler_params=pltpu.CompilerParams(vmem_limit_bytes=8 << 20),
        cost_estimate=pl.CostEstimate(flops=1 << 18, bytes_accessed=2 << 20, transcendentals=0),
        name=name,
    )(fields, labels, after)


def flow_kernel(total_rows, chunks, where_ref, mid_ref, before_ref, after_ref, out_ref, *state):
    hs, us, vs, qs, h1s = state
    lat = where_ref[0]
    last = where_ref[1]
    local_rows = mid_ref.shape[1]
    width = mid_ref.shape[2]
    strips = local_rows // STRIP + 2
    pad = STRIP

    def rows(s, shift=0):
        return pl.ds(pad + STRIP * s + shift, STRIP)

    zero = jnp.zeros((STRIP, width), jnp.float32)
    for ref in (hs, us, vs, qs, h1s):
        ref[0:pad, :] = zero
        ref[pad + STRIP * strips :, :] = zero
    for ref, field in ((hs, 0), (us, 1), (vs, 2), (qs, 3)):
        ref[pad + STRIP : pad + STRIP * (strips - 1), :] = mid_ref[field]
    for s, edge in ((0, before_ref), (strips - 1, after_ref)):
        vs[rows(s), :] = edge[0:8, :]
        hs[rows(s), :] = edge[8:16, :]
        us[rows(s), :] = edge[16:24, :]
    qs[rows(0), :] = pltpu.roll(before_ref[16:24, :], 5, 0)
    qs[rows(strips - 1), :] = pltpu.roll(after_ref[16:24, :], 3, 0)

    inside = [None] * strips
    inside[0] = jnp.where(lat > 0, 1.0, 0.0).astype(jnp.float32)
    inside[-1] = jnp.where(lat < last, 1.0, 0.0).astype(jnp.float32)

    def kept(value, s):
        return value if inside[s] is None else value * inside[s]

    lane_rows = lax.broadcasted_iota(jnp.int32, (STRIP, width), 0)

    def coriolis(s):
        row = (lane_rows + (lat * local_rows + STRIP * (s - 1))).astype(jnp.float32)
        return coriolis_coef * (2.0 * (row + 0.5) / total_rows - 1.0)

    for k in range(STEPS):
        final = k == STEPS - 1
        for s in range(strips):
            u = us[rows(s), :]
            h1s[rows(s), :] = kept(
                hs[rows(s), :]
                - depth_coef
                * ((east(u) - west(u)) + (vs[rows(s, 1), :] - vs[rows(s, -1), :])),
                s,
            )
        carried = qs[rows(0, -1), :]
        for s in range(1, strips - 1) if final else range(strips):
            f = coriolis(s)
            h1 = h1s[rows(s), :]
            v = vs[rows(s), :]
            u1 = us[rows(s), :] + f * v - grav_coef * (east(h1) - west(h1))
            v1 = v - f * u1 - grav_coef * (h1s[rows(s, 1), :] - h1s[rows(s, -1), :])
            q = qs[rows(s), :]
            if final:
                south = qs[rows(s, -1), :]
            else:
                south = carried
                if s < strips - 1:
                    carried = qs[rows(s + 1, -1), :]
            north = qs[rows(s, 1), :]
            e, w = east(q), west(q)
            q1 = (
                q
                - advect_coef * (u1 * (e - w) + v1 * (north - south))
                + diffuse_coef * ((e + w) + (north + south) - 4.0 * q)
            )
            if not final:
                us[rows(s), :] = kept(u1, s)
                vs[rows(s), :] = kept(v1, s)
                qs[rows(s), :] = kept(q1, s)
                hs[rows(s), :] = h1
            else:
                at = slice(STRIP * (s - 1), STRIP * s)
                for field, value in enumerate((h1, u1, v1, q1)):
                    if chunks == 1:
                        out_ref[field, at, :] = value
                    else:
                        size = width // chunks
                        for c in range(chunks):
                            out_ref[c, field, at, :] = value[:, c * size : (c + 1) * size]


def flow(where, middle, before, after, total_rows, chunks, name):
    fields, local_rows, width = middle.shape
    shape = (fields, local_rows, width)
    if chunks > 1:
        shape = (chunks, fields, local_rows, width // chunks)
    state = pltpu.VMEM((local_rows + 4 * STRIP, width), jnp.float32)
    return pl.pallas_call(
        functools.partial(flow_kernel, total_rows, chunks),
        out_shape=jax.ShapeDtypeStruct(shape, jnp.float32),
        in_specs=[SMEM, VMEM, VMEM, VMEM],
        out_specs=VMEM,
        scratch_shapes=[state] * 5,
        compiler_params=pltpu.CompilerParams(vmem_limit_bytes=24 << 20),
        cost_estimate=pl.CostEstimate(
            flops=60 * 10 * STRIP * width, bytes_accessed=1 << 22, transcendentals=0
        ),
        name=name,
    )(where, middle, before, after)


def pair_kernel(pairing_ref, all_ref, labels_ref, spread_ref):
    members, fields, local_rows, size = all_ref.shape
    tiles = size // TILE
    lane = lax.broadcasted_iota(jnp.int32, (REGIONS, TILE), 1)

    def folded(x):
        return x[:STRIP] + x[STRIP:]

    weights, counts = [], []
    shown = [
        [
            jnp.broadcast_to(labels_ref[i : i + local_rows, t : t + 1], (local_rows, TILE))
            for t in range(tiles)
        ]
        for i in range(3)
    ]
    for r in range(REGIONS):

        def is_r(x):
            return jnp.where(x == float(r + 1), 1.0, 0.0).astype(jnp.float32)

        count, weight = None, []
        for t in range(tiles):
            own = is_r(shown[1][t])
            count = folded(own) if count is None else count + folded(own)
            weight.append(0.125 * (is_r(shown[0][t]) + 2.0 * own + is_r(shown[2][t])))
        counts.append(jnp.sum(count, axis=0, keepdims=True))
        weights.append(weight)

    def column(rows):
        return jnp.sum(jnp.concatenate(rows, axis=0), axis=1, keepdims=True)

    empty = jnp.where(lane == 1, column(counts), 0.0)
    for m in range(members):
        partner = pairing_ref[m]
        squares = [None] * tiles
        for field in range(fields):
            spread = 0.5 * (all_ref[m, field] - all_ref[partner, field])
            for t in range(tiles):
                x = spread[:, t * TILE : (t + 1) * TILE]
                at = (field * tiles + t) * local_rows
                spread_ref[m, at : at + local_rows, :] = x
                squares[t] = x * x if squares[t] is None else squares[t] + x * x
        parts = []
        for weight in weights:
            part = None
            for t in range(tiles):
                y = folded(squares[t] * weight[t])
                part = y if part is None else part + y
            parts.append(jnp.sum(part, axis=0, keepdims=True))
        spread_ref[m, fields * tiles * local_rows :, :] = jnp.where(
            lane == 0, column(parts), empty
        )


def pair_spread(pairing, everyone, labels):
    members, fields, local_rows, size = everyone.shape
    rows = fields * local_rows * size // TILE + REGIONS
    return pl.pallas_call(
        pair_kernel,
        out_shape=jax.ShapeDtypeStruct((members, rows, TILE), jnp.float32),
        in_specs=[SMEM, VMEM, VMEM],
        out_specs=VMEM,
        compiler_params=pltpu.CompilerParams(vmem_limit_bytes=8 << 20),
        cost_estimate=pl.CostEstimate(flops=1 << 20, bytes_accessed=3 << 20, transcendentals=0),
        name="pair_spread",
    )(pairing, everyone, labels)


def spread_edge_kernel(shape, back_ref, up_ref, down_ref, share_ref):
    fields, local_rows, width = shape
    chunks = back_ref.shape[0]
    tiles = width // chunks // TILE
    tail = fields * tiles * local_rows
    share = back_ref[0, tail:, :]
    for c in range(1, chunks):
        share = share + back_ref[c, tail:, :]
    for i in range(share_ref.shape[0]):
        share_ref[i] = share
    for c in range(chunks):
        for t in range(tiles):
            tile = c * tiles + t
            at = slice(tile * TILE, (tile + 1) * TILE)
            values = []
            for i in range(fields):
                row = (i * tiles + t) * local_rows
                values.append(back_ref[c, row : row + local_rows, :])
            pack_rows(up_ref, down_ref, at, *values)


def spread_edges(back, shape, lat_size):
    edge = jax.ShapeDtypeStruct((3 * STRIP, shape[2]), jnp.float32)
    return pl.pallas_call(
        functools.partial(spread_edge_kernel, shape),
        out_shape=(edge, edge, jax.ShapeDtypeStruct((lat_size, REGIONS, TILE), jnp.float32)),
        in_specs=[VMEM],
        out_specs=(VMEM,) * 3,
        compiler_params=pltpu.CompilerParams(vmem_limit_bytes=8 << 20),
        cost_estimate=pl.CostEstimate(flops=1 << 18, bytes_accessed=2 << 20, transcendentals=0),
        name="spread_edges",
    )(back)


def recentre_kernel(
    labels_ref, analysis_ref, a_before_ref, a_after_ref, back_ref, b_before_ref, b_after_ref,
    shares_ref, mid_ref, before_ref, after_ref, factor_ref
):
    chunks = back_ref.shape[0]
    fields, local_rows, width = analysis_ref.shape
    tiles = width // chunks // TILE
    sums = jnp.sum(shares_ref[...], axis=0)
    region_sum = jnp.broadcast_to(sums[:, 0:1], (REGIONS, TILE))
    cells = jnp.broadcast_to(sums[:, 1:2], (REGIONS, TILE))
    factor = target_size / jnp.sqrt(region_sum / cells + small_eps)
    factor_ref[...] = factor

    def scale_of(labels):
        scale = jnp.zeros(labels.shape, jnp.float32)
        for r in range(REGIONS):
            scale = jnp.where(labels == float(r + 1), factor[r : r + 1, :], scale)
        return scale

    def rows_of(ref, row):
        parts = [ref[row : row + 1, k * TILE : (k + 1) * TILE] for k in range(STRIP)]
        return jnp.concatenate(parts, axis=0)

    scale = scale_of(labels_ref[...])
    below = scale_of(rows_of(a_before_ref, 8))
    above = scale_of(rows_of(a_after_ref, 15))
    row = lax.broadcasted_iota(jnp.int32, (STRIP, TILE), 0)
    below_uq = jnp.where(row < 3, pltpu.roll(below, 3, 0), below)
    above_uq = jnp.where(row >= 5, pltpu.roll(above, 5, 0), above)

    for c in range(chunks):
        for t in range(tiles):
            tile = c * tiles + t
            at = slice(tile * TILE, (tile + 1) * TILE)

            def wide(x):
                return jnp.broadcast_to(x[:, tile : tile + 1], (x.shape[0], TILE))

            own = wide(scale)
            for i in range(fields):
                first = (i * tiles + t) * local_rows
                mid_ref[i, :, at] = (
                    analysis_ref[i, :, at] + own * back_ref[c, first : first + local_rows, :]
                )
            for out, a_ref, b_ref, near, mixed in (
                (before_ref, a_before_ref, b_before_ref, below, below_uq),
                (after_ref, a_after_ref, b_after_ref, above, above_uq),
            ):
                near = wide(near)
                for rows, factor_rows in ((0, near), (8, near), (16, wide(mixed))):
                    pack = slice(rows, rows + STRIP)
                    out[pack, at] = a_ref[pack, at] + factor_rows * b_ref[pack, at]


def recentre(labels, analysis, a_before, a_after, back, b_before, b_after, shares):
    edge = jax.ShapeDtypeStruct(a_before.shape, jnp.float32)
    return pl.pallas_call(
        recentre_kernel,
        out_shape=(
            jax.ShapeDtypeStruct(analysis.shape, jnp.float32),
            edge,
            edge,
            jax.ShapeDtypeStruct((REGIONS, TILE), jnp.float32),
        ),
        in_specs=[VMEM] * 8,
        out_specs=(VMEM,) * 4,
        compiler_params=pltpu.CompilerParams(vmem_limit_bytes=16 << 20),
        cost_estimate=pl.CostEstimate(flops=1 << 20, bytes_accessed=4 << 20, transcendentals=0),
        name="recentre",
    )(labels, analysis, a_before, a_after, back, b_before, b_after, shares)


def local(replica_variables, analysis, labels, pairing):
    members = lax.axis_size("mem")
    lat_size = lax.axis_size("lat")
    lat = lax.axis_index("lat")
    member = lax.axis_index("mem")
    x = replica_variables[0]
    fields, local_rows, width = x.shape
    tiles = width // members // TILE
    total_rows = float(local_rows * lat_size)
    where = jnp.stack([lat, jnp.int32(lat_size - 1)]).astype(jnp.int32)
    up = [(i, i + 1) for i in range(lat_size - 1)]
    down = [(j, i) for i, j in up]

    coded = (labels + 1).astype(jnp.float32)
    coded = jnp.pad(coded, ((0, 0), (0, TILE - labels.shape[1])))
    last, first = packed_edges(x, coded, coded, 1, "packed_edges")
    before = lax.ppermute(last, "lat", up)
    after = lax.ppermute(first, "lat", down)
    last, first = packed_edges(analysis, coded, before, STRIP, "analysis_edges")
    a_before = lax.ppermute(last, "lat", up)
    a_after = lax.ppermute(first, "lat", down)
    pieces = flow(where, x, before, after, total_rows, members, "first_flow")
    everyone = lax.all_to_all(pieces, "mem", 0, 0, tiled=True)

    rows = jnp.concatenate([before[8:9, :TILE], coded, after[15:16, :TILE]], axis=0)
    own = lax.dynamic_slice_in_dim(rows, member * tiles, tiles, axis=1)
    own = jnp.pad(own, ((0, 6), (0, TILE - tiles)))
    spread = pair_spread(pairing, everyone, own)
    back = lax.all_to_all(spread, "mem", 0, 0, tiled=True)
    last, first, share = spread_edges(back, x.shape, lat_size)
    b_before = lax.ppermute(last, "lat", up)
    b_after = lax.ppermute(first, "lat", down)
    shares = lax.all_to_all(share, "lat", 0, 0, tiled=True)
    middle, before, after, factor = recentre(
        coded, analysis, a_before, a_after, back, b_before, b_after, shares
    )
    closing = flow(where, middle, before, after, total_rows, 1, "closing_flow")
    return closing[None], factor[:, 0].reshape(1, REGIONS)


def solution(mesh):
    return jax.shard_map(
        local,
        mesh=mesh,
        in_specs=(P("mem", None, "lat", None), P(None, "lat", None), P("lat", None), P()),
        out_specs=(P("mem", None, "lat", None), P("mem", None)),
        check_vma=False,
    )
```

```python
import functools

import jax
import jax.numpy as jnp
from jax import lax
from jax.experimental import pallas as pl
from jax.experimental.pallas import tpu as pltpu
from jax.sharding import PartitionSpec as P

TILE = 128
REGIONS = 8
STEPS = 3
STRIP = 8
PARTS = 8

grav_coef = 0.1
depth_coef = 0.1
advect_coef = 0.05
diffuse_coef = 0.05
coriolis_coef = 0.05
target_size = 0.5
small_eps = 1e-06

VMEM = pl.BlockSpec(memory_space=pltpu.VMEM)
SMEM = pl.BlockSpec(memory_space=pltpu.SMEM)


def east(field):
    return pltpu.roll(field, field.shape[1] - 1, 1)


def west(field):
    return pltpu.roll(field, 1, 1)


def pack_rows(up_ref, down_ref, at, h, u, v, q):
    row = lax.broadcasted_iota(jnp.int32, (STRIP, v.shape[1]), 0)
    up_ref[0:8, at] = v[8:16]
    up_ref[8:16, at] = h[8:16]
    up_ref[16:24, at] = jnp.where(row < 3, pltpu.roll(q[8:16], 3, 0), u[8:16])
    down_ref[0:8, at] = v[0:8]
    down_ref[8:16, at] = h[0:8]
    down_ref[16:24, at] = jnp.where(row >= 5, pltpu.roll(q[0:8], 5, 0), u[0:8])


def first_edge_kernel(fields_ref, labels_ref, up_ref, down_ref, coded_ref):
    width = fields_ref.shape[2]
    size = width // PARTS
    for c in range(PARTS):
        at = slice(c * size, (c + 1) * size)
        pack_rows(up_ref, down_ref, at, *[fields_ref[i, :, at] for i in range(4)])
    local_rows, columns = labels_ref.shape
    coded_ref[...] = jnp.zeros(coded_ref.shape, jnp.float32)
    coded_ref[:, 0:columns] = labels_ref[...].astype(jnp.float32) + 1.0
    up_ref[8:9, 0:TILE] = coded_ref[local_rows - 1 :, :]
    down_ref[15:16, 0:TILE] = coded_ref[0:1, :]


def first_edges(fields, labels):
    edge = jax.ShapeDtypeStruct((3 * STRIP, fields.shape[2]), jnp.float32)
    return pl.pallas_call(
        first_edge_kernel,
        out_shape=(edge, edge, jax.ShapeDtypeStruct((labels.shape[0], TILE), jnp.float32)),
        in_specs=[VMEM] * 2,
        out_specs=(VMEM,) * 3,
        compiler_params=pltpu.CompilerParams(vmem_limit_bytes=8 << 20),
        cost_estimate=pl.CostEstimate(flops=1 << 18, bytes_accessed=2 << 20, transcendentals=0),
        name="first_edges",
    )(fields, labels)


def edge_kernel(fields_ref, labels_ref, after_ref, up_ref, down_ref):
    width = fields_ref.shape[2]
    size = width // PARTS
    for c in range(PARTS):
        at = slice(c * size, (c + 1) * size)
        pack_rows(up_ref, down_ref, at, *[fields_ref[i, :, at] for i in range(4)])
    for k in range(STRIP):
        at = slice(k * TILE, (k + 1) * TILE)
        row = labels_ref.shape[0] - STRIP + k
        up_ref[8:9, at] = labels_ref[row : row + 1, :]
        down_ref[15:16, at] = labels_ref[k : k + 1, :]


def packed_edges(fields, labels, after):
    edge = jax.ShapeDtypeStruct((3 * STRIP, fields.shape[2]), jnp.float32)
    return pl.pallas_call(
        edge_kernel,
        out_shape=(edge, edge),
        in_specs=[VMEM, VMEM, pl.BlockSpec(memory_space=pl.ANY)],
        out_specs=(VMEM, VMEM),
        compiler_params=pltpu.CompilerParams(vmem_limit_bytes=8 << 20),
        cost_estimate=pl.CostEstimate(flops=1 << 18, bytes_accessed=2 << 20, transcendentals=0),
        name="analysis_edges",
    )(fields, labels, after)


def flow_kernel(total_rows, chunks, where_ref, mid_ref, before_ref, after_ref, out_ref, *state):
    hs, us, vs, qs, h1s = state
    lat = where_ref[0]
    last = where_ref[1]
    local_rows = mid_ref.shape[1]
    width = mid_ref.shape[2]
    strips = local_rows // STRIP + 2
    pad = STRIP

    def rows(s, shift=0):
        return pl.ds(pad + STRIP * s + shift, STRIP)

    zero = jnp.zeros((STRIP, width), jnp.float32)
    for ref in (hs, us, vs, qs, h1s):
        ref[0:pad, :] = zero
        ref[pad + STRIP * strips :, :] = zero
    for ref, field in ((hs, 0), (us, 1), (vs, 2), (qs, 3)):
        ref[pad + STRIP : pad + STRIP * (strips - 1), :] = mid_ref[field]
    for s, edge in ((0, before_ref), (strips - 1, after_ref)):
        vs[rows(s), :] = edge[0:8, :]
        hs[rows(s), :] = edge[8:16, :]
        us[rows(s), :] = edge[16:24, :]
    qs[rows(0), :] = pltpu.roll(before_ref[16:24, :], 5, 0)
    qs[rows(strips - 1), :] = pltpu.roll(after_ref[16:24, :], 3, 0)

    inside = [None] * strips
    inside[0] = jnp.where(lat > 0, 1.0, 0.0).astype(jnp.float32)
    inside[-1] = jnp.where(lat < last, 1.0, 0.0).astype(jnp.float32)

    def kept(value, s):
        return value if inside[s] is None else value * inside[s]

    lane_rows = lax.broadcasted_iota(jnp.int32, (STRIP, width), 0)

    def coriolis(s):
        row = (lane_rows + (lat * local_rows + STRIP * (s - 1))).astype(jnp.float32)
        return coriolis_coef * (2.0 * (row + 0.5) / total_rows - 1.0)

    for k in range(STEPS):
        final = k == STEPS - 1
        for s in range(strips):
            u = us[rows(s), :]
            h1s[rows(s), :] = kept(
                hs[rows(s), :]
                - depth_coef
                * ((east(u) - west(u)) + (vs[rows(s, 1), :] - vs[rows(s, -1), :])),
                s,
            )
        carried = qs[rows(0, -1), :]
        for s in range(1, strips - 1) if final else range(strips):
            f = coriolis(s)
            h1 = h1s[rows(s), :]
            v = vs[rows(s), :]
            u1 = us[rows(s), :] + f * v - grav_coef * (east(h1) - west(h1))
            v1 = v - f * u1 - grav_coef * (h1s[rows(s, 1), :] - h1s[rows(s, -1), :])
            q = qs[rows(s), :]
            if final:
                south = qs[rows(s, -1), :]
            else:
                south = carried
                if s < strips - 1:
                    carried = qs[rows(s + 1, -1), :]
            north = qs[rows(s, 1), :]
            e, w = east(q), west(q)
            q1 = (
                q
                - advect_coef * (u1 * (e - w) + v1 * (north - south))
                + diffuse_coef * ((e + w) + (north + south) - 4.0 * q)
            )
            if not final:
                us[rows(s), :] = kept(u1, s)
                vs[rows(s), :] = kept(v1, s)
                qs[rows(s), :] = kept(q1, s)
                hs[rows(s), :] = h1
            else:
                at = slice(STRIP * (s - 1), STRIP * s)
                for field, value in enumerate((h1, u1, v1, q1)):
                    if chunks == 1:
                        out_ref[field, at, :] = value
                    else:
                        size = width // chunks
                        for c in range(chunks):
                            out_ref[c, field, at, :] = value[:, c * size : (c + 1) * size]


def flow(where, middle, before, after, total_rows, chunks, name):
    fields, local_rows, width = middle.shape
    shape = (fields, local_rows, width)
    if chunks > 1:
        shape = (chunks, fields, local_rows, width // chunks)
    state = pltpu.VMEM((local_rows + 4 * STRIP, width), jnp.float32)
    return pl.pallas_call(
        functools.partial(flow_kernel, total_rows, chunks),
        out_shape=jax.ShapeDtypeStruct(shape, jnp.float32),
        in_specs=[SMEM, VMEM, VMEM, VMEM],
        out_specs=VMEM,
        scratch_shapes=[state] * 5,
        compiler_params=pltpu.CompilerParams(vmem_limit_bytes=24 << 20),
        cost_estimate=pl.CostEstimate(
            flops=60 * 10 * STRIP * width, bytes_accessed=1 << 22, transcendentals=0
        ),
        name=name,
    )(where, middle, before, after)


def pair_kernel(
    where_ref, pairing_ref, all_ref, labels_ref, before_ref, after_ref, spread_ref, near_ref
):
    members, fields, local_rows, size = all_ref.shape
    tiles = size // TILE
    lane = lax.broadcasted_iota(jnp.int32, (REGIONS, TILE), 1)

    def folded(x):
        return x[:STRIP] + x[STRIP:]

    weights, counts = [], []
    near_ref[0:STRIP, :] = jnp.broadcast_to(before_ref[8:9, 0:TILE], (STRIP, TILE))
    near_ref[STRIP : STRIP + local_rows, :] = labels_ref[...]
    near_ref[STRIP + local_rows :, :] = jnp.broadcast_to(after_ref[15:16, 0:TILE], (STRIP, TILE))
    column_of = lax.broadcasted_iota(jnp.int32, (local_rows, TILE), 1)
    shown = []
    for i in range(3):
        near = near_ref[STRIP - 1 + i : STRIP - 1 + i + local_rows, :]
        shown.append([])
        for t in range(tiles):
            own = jnp.where(column_of == where_ref[2] * tiles + t, near, 0.0)
            own = jnp.sum(own, axis=1, keepdims=True)
            shown[-1].append(jnp.broadcast_to(own, (local_rows, TILE)))
    for r in range(REGIONS):

        def is_r(x):
            return jnp.where(x == float(r + 1), 1.0, 0.0).astype(jnp.float32)

        count, weight = None, []
        for t in range(tiles):
            own = is_r(shown[1][t])
            count = folded(own) if count is None else count + folded(own)
            weight.append(0.125 * (is_r(shown[0][t]) + 2.0 * own + is_r(shown[2][t])))
        counts.append(jnp.sum(count, axis=0, keepdims=True))
        weights.append(weight)

    def column(rows):
        return jnp.sum(jnp.concatenate(rows, axis=0), axis=1, keepdims=True)

    empty = jnp.where(lane == 1, column(counts), 0.0)
    for m in range(members):
        partner = pairing_ref[m]
        squares = [None] * tiles
        for field in range(fields):
            spread = 0.5 * (all_ref[m, field] - all_ref[partner, field])
            for t in range(tiles):
                x = spread[:, t * TILE : (t + 1) * TILE]
                at = (field * tiles + t) * local_rows
                spread_ref[m, at : at + local_rows, :] = x
                squares[t] = x * x if squares[t] is None else squares[t] + x * x
        parts = []
        for weight in weights:
            part = None
            for t in range(tiles):
                y = folded(squares[t] * weight[t])
                part = y if part is None else part + y
            parts.append(jnp.sum(part, axis=0, keepdims=True))
        spread_ref[m, fields * tiles * local_rows :, :] = jnp.where(
            lane == 0, column(parts), empty
        )


def pair_spread(where, pairing, everyone, labels, before, after):
    members, fields, local_rows, size = everyone.shape
    rows = fields * local_rows * size // TILE + REGIONS
    return pl.pallas_call(
        pair_kernel,
        out_shape=jax.ShapeDtypeStruct((members, rows, TILE), jnp.float32),
        in_specs=[SMEM, SMEM, VMEM, VMEM, VMEM, VMEM],
        out_specs=VMEM,
        scratch_shapes=[pltpu.VMEM((local_rows + 2 * STRIP, TILE), jnp.float32)],
        compiler_params=pltpu.CompilerParams(vmem_limit_bytes=8 << 20),
        cost_estimate=pl.CostEstimate(flops=1 << 20, bytes_accessed=3 << 20, transcendentals=0),
        name="pair_spread",
    )(where, pairing, everyone, labels, before, after)


def spread_edge_kernel(shape, back_ref, up_ref, down_ref, share_ref):
    fields, local_rows, width = shape
    chunks = back_ref.shape[0]
    tiles = width // chunks // TILE
    tail = fields * tiles * local_rows
    share = back_ref[0, tail:, :]
    for c in range(1, chunks):
        share = share + back_ref[c, tail:, :]
    for i in range(share_ref.shape[0]):
        share_ref[i] = share
    for c in range(chunks):
        for t in range(tiles):
            tile = c * tiles + t
            at = slice(tile * TILE, (tile + 1) * TILE)
            values = []
            for i in range(fields):
                row = (i * tiles + t) * local_rows
                values.append(back_ref[c, row : row + local_rows, :])
            pack_rows(up_ref, down_ref, at, *values)


def spread_edges(back, shape, lat_size):
    edge = jax.ShapeDtypeStruct((3 * STRIP, shape[2]), jnp.float32)
    return pl.pallas_call(
        functools.partial(spread_edge_kernel, shape),
        out_shape=(edge, edge, jax.ShapeDtypeStruct((lat_size, REGIONS, TILE), jnp.float32)),
        in_specs=[VMEM],
        out_specs=(VMEM,) * 3,
        compiler_params=pltpu.CompilerParams(vmem_limit_bytes=8 << 20),
        cost_estimate=pl.CostEstimate(flops=1 << 18, bytes_accessed=2 << 20, transcendentals=0),
        name="spread_edges",
    )(back)


def recentre_kernel(
    labels_ref, analysis_ref, a_before_ref, a_after_ref, back_ref, b_before_ref, b_after_ref,
    shares_ref, mid_ref, before_ref, after_ref, factor_ref
):
    chunks = back_ref.shape[0]
    fields, local_rows, width = analysis_ref.shape
    tiles = width // chunks // TILE
    sums = jnp.sum(shares_ref[...], axis=0)
    region_sum = jnp.broadcast_to(sums[:, 0:1], (REGIONS, TILE))
    cells = jnp.broadcast_to(sums[:, 1:2], (REGIONS, TILE))
    factor = target_size / jnp.sqrt(region_sum / cells + small_eps)
    diagonal = lax.broadcasted_iota(jnp.int32, factor.shape, 0) == lax.broadcasted_iota(
        jnp.int32, factor.shape, 1
    )
    in_lanes = jnp.sum(jnp.where(diagonal, factor, 0.0), axis=0, keepdims=True)
    factor_ref[...] = in_lanes[:, 0:REGIONS]

    def scale_of(labels):
        scale = jnp.zeros(labels.shape, jnp.float32)
        for r in range(REGIONS):
            scale = jnp.where(labels == float(r + 1), factor[r : r + 1, :], scale)
        return scale

    def rows_of(ref, row):
        parts = [ref[row : row + 1, k * TILE : (k + 1) * TILE] for k in range(STRIP)]
        return jnp.concatenate(parts, axis=0)

    scale = scale_of(labels_ref[...])
    below = scale_of(rows_of(a_before_ref, 8))
    above = scale_of(rows_of(a_after_ref, 15))
    row = lax.broadcasted_iota(jnp.int32, (STRIP, TILE), 0)
    below_uq = jnp.where(row < 3, pltpu.roll(below, 3, 0), below)
    above_uq = jnp.where(row >= 5, pltpu.roll(above, 5, 0), above)

    for c in range(chunks):
        for t in range(tiles):
            tile = c * tiles + t
            at = slice(tile * TILE, (tile + 1) * TILE)

            def wide(x):
                return jnp.broadcast_to(x[:, tile : tile + 1], (x.shape[0], TILE))

            own = wide(scale)
            for i in range(fields):
                first = (i * tiles + t) * local_rows
                mid_ref[i, :, at] = (
                    analysis_ref[i, :, at] + own * back_ref[c, first : first + local_rows, :]
                )
            for out, a_ref, b_ref, near, mixed in (
                (before_ref, a_before_ref, b_before_ref, below, below_uq),
                (after_ref, a_after_ref, b_after_ref, above, above_uq),
            ):
                near = wide(near)
                for rows, factor_rows in ((0, near), (8, near), (16, wide(mixed))):
                    pack = slice(rows, rows + STRIP)
                    out[pack, at] = a_ref[pack, at] + factor_rows * b_ref[pack, at]


def recentre(labels, analysis, a_before, a_after, back, b_before, b_after, shares):
    edge = jax.ShapeDtypeStruct(a_before.shape, jnp.float32)
    return pl.pallas_call(
        recentre_kernel,
        out_shape=(
            jax.ShapeDtypeStruct(analysis.shape, jnp.float32),
            edge,
            edge,
            jax.ShapeDtypeStruct((1, REGIONS), jnp.float32),
        ),
        in_specs=[VMEM] * 8,
        out_specs=(VMEM,) * 4,
        compiler_params=pltpu.CompilerParams(vmem_limit_bytes=16 << 20),
        cost_estimate=pl.CostEstimate(flops=1 << 20, bytes_accessed=4 << 20, transcendentals=0),
        name="recentre",
    )(labels, analysis, a_before, a_after, back, b_before, b_after, shares)


def local(replica_variables, analysis, labels, pairing):
    members = lax.axis_size("mem")
    lat_size = lax.axis_size("lat")
    lat = lax.axis_index("lat")
    member = lax.axis_index("mem")
    x = replica_variables[0]
    fields, local_rows, width = x.shape
    total_rows = float(local_rows * lat_size)
    where = jnp.stack([lat, jnp.int32(lat_size - 1), member]).astype(jnp.int32)
    up = [(i, i + 1) for i in range(lat_size - 1)]
    down = [(j, i) for i, j in up]

    last, first, coded = first_edges(x, labels)
    before = lax.ppermute(last, "lat", up)
    after = lax.ppermute(first, "lat", down)
    last, first = packed_edges(analysis, coded, before)
    a_before = lax.ppermute(last, "lat", up)
    a_after = lax.ppermute(first, "lat", down)
    pieces = flow(where, x, before, after, total_rows, members, "first_flow")
    everyone = lax.all_to_all(pieces, "mem", 0, 0, tiled=True)

    spread = pair_spread(where, pairing, everyone, coded, before, after)
    back = lax.all_to_all(spread, "mem", 0, 0, tiled=True)
    last, first, share = spread_edges(back, x.shape, lat_size)
    b_before = lax.ppermute(last, "lat", up)
    b_after = lax.ppermute(first, "lat", down)
    shares = lax.all_to_all(share, "lat", 0, 0, tiled=True)
    middle, before, after, factor = recentre(
        coded, analysis, a_before, a_after, back, b_before, b_after, shares
    )
    closing = flow(where, middle, before, after, total_rows, 1, "closing_flow")
    return closing[None], factor


def solution(mesh):
    return jax.shard_map(
        local,
        mesh=mesh,
        in_specs=(P("mem", None, "lat", None), P(None, "lat", None), P("lat", None), P()),
        out_specs=(P("mem", None, "lat", None), P("mem", None)),
        check_vma=False,
    )
```

```python
import functools

import jax
import jax.numpy as jnp
from jax import lax
from jax.experimental import pallas as pl
from jax.experimental.pallas import tpu as pltpu
from jax.sharding import PartitionSpec as P

TILE = 128
REGIONS = 8
STEPS = 3
STRIP = 8
PARTS = 8

grav_coef = 0.1
depth_coef = 0.1
advect_coef = 0.05
diffuse_coef = 0.05
coriolis_coef = 0.05
target_size = 0.5
small_eps = 1e-06

VMEM = pl.BlockSpec(memory_space=pltpu.VMEM)
SMEM = pl.BlockSpec(memory_space=pltpu.SMEM)


def east(field):
    return pltpu.roll(field, field.shape[1] - 1, 1)


def west(field):
    return pltpu.roll(field, 1, 1)


def pack_rows(up_ref, down_ref, at, h, u, v, q):
    row = lax.broadcasted_iota(jnp.int32, (STRIP, v.shape[1]), 0)
    up_ref[0:8, at] = v[8:16]
    up_ref[8:16, at] = h[8:16]
    up_ref[16:24, at] = jnp.where(row < 3, pltpu.roll(q[8:16], 3, 0), u[8:16])
    down_ref[0:8, at] = v[0:8]
    down_ref[8:16, at] = h[0:8]
    down_ref[16:24, at] = jnp.where(row >= 5, pltpu.roll(q[0:8], 5, 0), u[0:8])


def first_edge_kernel(fields_ref, labels_ref, up_ref, down_ref, coded_ref):
    width = fields_ref.shape[2]
    size = width // PARTS
    for c in range(PARTS):
        at = slice(c * size, (c + 1) * size)
        pack_rows(up_ref, down_ref, at, *[fields_ref[i, :, at] for i in range(4)])
    local_rows, columns = labels_ref.shape
    coded_ref[...] = jnp.zeros(coded_ref.shape, jnp.float32)
    coded_ref[:, 0:columns] = labels_ref[...].astype(jnp.float32) + 1.0
    up_ref[8:9, 0:TILE] = coded_ref[local_rows - 1 :, :]
    down_ref[15:16, 0:TILE] = coded_ref[0:1, :]


def first_edges(fields, labels):
    edge = jax.ShapeDtypeStruct((3 * STRIP, fields.shape[2]), jnp.float32)
    return pl.pallas_call(
        first_edge_kernel,
        out_shape=(edge, edge, jax.ShapeDtypeStruct((labels.shape[0], TILE), jnp.float32)),
        in_specs=[VMEM] * 2,
        out_specs=(VMEM,) * 3,
        compiler_params=pltpu.CompilerParams(vmem_limit_bytes=6 << 20),
        cost_estimate=pl.CostEstimate(flops=1 << 18, bytes_accessed=2 << 20, transcendentals=0),
        name="first_edges",
    )(fields, labels)


def edge_kernel(fields_ref, labels_ref, after_ref, up_ref, down_ref):
    width = fields_ref.shape[2]
    size = width // PARTS
    for c in range(PARTS):
        at = slice(c * size, (c + 1) * size)
        pack_rows(up_ref, down_ref, at, *[fields_ref[i, :, at] for i in range(4)])
    for k in range(STRIP):
        at = slice(k * TILE, (k + 1) * TILE)
        row = labels_ref.shape[0] - STRIP + k
        up_ref[8:9, at] = labels_ref[row : row + 1, :]
        down_ref[15:16, at] = labels_ref[k : k + 1, :]


def packed_edges(fields, labels, after):
    edge = jax.ShapeDtypeStruct((3 * STRIP, fields.shape[2]), jnp.float32)
    return pl.pallas_call(
        edge_kernel,
        out_shape=(edge, edge),
        in_specs=[VMEM, VMEM, pl.BlockSpec(memory_space=pl.ANY)],
        out_specs=(VMEM, VMEM),
        compiler_params=pltpu.CompilerParams(vmem_limit_bytes=6 << 20),
        cost_estimate=pl.CostEstimate(flops=1 << 18, bytes_accessed=2 << 20, transcendentals=0),
        name="analysis_edges",
    )(fields, labels, after)


def flow_kernel(total_rows, chunks, where_ref, mid_ref, before_ref, after_ref, out_ref, *state):
    hs, us, vs, qs, h1s = state
    lat = where_ref[0]
    last = where_ref[1]
    local_rows = mid_ref.shape[1]
    width = mid_ref.shape[2]
    strips = local_rows // STRIP + 2
    pad = STRIP

    def rows(s, shift=0):
        return pl.ds(pad + STRIP * s + shift, STRIP)

    zero = jnp.zeros((STRIP, width), jnp.float32)
    for ref in (hs, us, vs, qs, h1s):
        ref[0:pad, :] = zero
        ref[pad + STRIP * strips :, :] = zero
    for ref, field in ((hs, 0), (us, 1), (vs, 2), (qs, 3)):
        ref[pad + STRIP : pad + STRIP * (strips - 1), :] = mid_ref[field]
    for s, edge in ((0, before_ref), (strips - 1, after_ref)):
        vs[rows(s), :] = edge[0:8, :]
        hs[rows(s), :] = edge[8:16, :]
        us[rows(s), :] = edge[16:24, :]
    qs[rows(0), :] = pltpu.roll(before_ref[16:24, :], 5, 0)
    qs[rows(strips - 1), :] = pltpu.roll(after_ref[16:24, :], 3, 0)

    inside = [None] * strips
    inside[0] = jnp.where(lat > 0, 1.0, 0.0).astype(jnp.float32)
    inside[-1] = jnp.where(lat < last, 1.0, 0.0).astype(jnp.float32)

    def kept(value, s):
        return value if inside[s] is None else value * inside[s]

    lane_rows = lax.broadcasted_iota(jnp.int32, (STRIP, width), 0)

    def coriolis(s):
        row = (lane_rows + (lat * local_rows + STRIP * (s - 1))).astype(jnp.float32)
        return coriolis_coef * (2.0 * (row + 0.5) / total_rows - 1.0)

    for k in range(STEPS):
        final = k == STEPS - 1
        for s in range(strips):
            u = us[rows(s), :]
            h1s[rows(s), :] = kept(
                hs[rows(s), :]
                - depth_coef
                * ((east(u) - west(u)) + (vs[rows(s, 1), :] - vs[rows(s, -1), :])),
                s,
            )
        carried = qs[rows(0, -1), :]
        for s in range(1, strips - 1) if final else range(strips):
            f = coriolis(s)
            h1 = h1s[rows(s), :]
            v = vs[rows(s), :]
            u1 = us[rows(s), :] + f * v - grav_coef * (east(h1) - west(h1))
            v1 = v - f * u1 - grav_coef * (h1s[rows(s, 1), :] - h1s[rows(s, -1), :])
            q = qs[rows(s), :]
            if final:
                south = qs[rows(s, -1), :]
            else:
                south = carried
                if s < strips - 1:
                    carried = qs[rows(s + 1, -1), :]
            north = qs[rows(s, 1), :]
            e, w = east(q), west(q)
            q1 = (
                q
                - advect_coef * (u1 * (e - w) + v1 * (north - south))
                + diffuse_coef * ((e + w) + (north + south) - 4.0 * q)
            )
            if not final:
                us[rows(s), :] = kept(u1, s)
                vs[rows(s), :] = kept(v1, s)
                qs[rows(s), :] = kept(q1, s)
                hs[rows(s), :] = h1
            else:
                at = slice(STRIP * (s - 1), STRIP * s)
                for field, value in enumerate((h1, u1, v1, q1)):
                    if chunks == 1:
                        out_ref[field, at, :] = value
                    else:
                        size = width // chunks
                        for c in range(chunks):
                            out_ref[c, field, at, :] = value[:, c * size : (c + 1) * size]


def flow(where, middle, before, after, total_rows, chunks, name):
    fields, local_rows, width = middle.shape
    shape = (fields, local_rows, width)
    if chunks > 1:
        shape = (chunks, fields, local_rows, width // chunks)
    state = pltpu.VMEM((local_rows + 4 * STRIP, width), jnp.float32)
    return pl.pallas_call(
        functools.partial(flow_kernel, total_rows, chunks),
        out_shape=jax.ShapeDtypeStruct(shape, jnp.float32),
        in_specs=[SMEM, VMEM, VMEM, VMEM],
        out_specs=VMEM,
        scratch_shapes=[state] * 5,
        compiler_params=pltpu.CompilerParams(vmem_limit_bytes=6 << 20),
        cost_estimate=pl.CostEstimate(
            flops=60 * 10 * STRIP * width, bytes_accessed=1 << 22, transcendentals=0
        ),
        name=name,
    )(where, middle, before, after)


def pair_kernel(
    where_ref, pairing_ref, all_ref, labels_ref, before_ref, after_ref, spread_ref, near_ref
):
    members, fields, local_rows, size = all_ref.shape
    tiles = size // TILE
    lane = lax.broadcasted_iota(jnp.int32, (REGIONS, TILE), 1)

    def folded(x):
        return x[:STRIP] + x[STRIP:]

    weights, counts = [], []
    near_ref[0:STRIP, :] = jnp.broadcast_to(before_ref[8:9, 0:TILE], (STRIP, TILE))
    near_ref[STRIP : STRIP + local_rows, :] = labels_ref[...]
    near_ref[STRIP + local_rows :, :] = jnp.broadcast_to(after_ref[15:16, 0:TILE], (STRIP, TILE))
    column_of = lax.broadcasted_iota(jnp.int32, (local_rows, TILE), 1)
    shown = []
    for i in range(3):
        near = near_ref[STRIP - 1 + i : STRIP - 1 + i + local_rows, :]
        shown.append([])
        for t in range(tiles):
            own = jnp.where(column_of == where_ref[2] * tiles + t, near, 0.0)
            own = jnp.sum(own, axis=1, keepdims=True)
            shown[-1].append(jnp.broadcast_to(own, (local_rows, TILE)))
    for r in range(REGIONS):

        def is_r(x):
            return jnp.where(x == float(r + 1), 1.0, 0.0).astype(jnp.float32)

        count, weight = None, []
        for t in range(tiles):
            own = is_r(shown[1][t])
            count = folded(own) if count is None else count + folded(own)
            weight.append(0.125 * (is_r(shown[0][t]) + 2.0 * own + is_r(shown[2][t])))
        counts.append(jnp.sum(count, axis=0, keepdims=True))
        weights.append(weight)

    def column(rows):
        return jnp.sum(jnp.concatenate(rows, axis=0), axis=1, keepdims=True)

    empty = jnp.where(lane == 1, column(counts), 0.0)
    for m in range(members):
        partner = pairing_ref[m]
        squares = [None] * tiles
        for field in range(fields):
            spread = 0.5 * (all_ref[m, field] - all_ref[partner, field])
            for t in range(tiles):
                x = spread[:, t * TILE : (t + 1) * TILE]
                at = (field * tiles + t) * local_rows
                spread_ref[m, at : at + local_rows, :] = x
                squares[t] = x * x if squares[t] is None else squares[t] + x * x
        parts = []
        for weight in weights:
            part = None
            for t in range(tiles):
                y = folded(squares[t] * weight[t])
                part = y if part is None else part + y
            parts.append(jnp.sum(part, axis=0, keepdims=True))
        spread_ref[m, fields * tiles * local_rows :, :] = jnp.where(
            lane == 0, column(parts), empty
        )


def pair_spread(where, pairing, everyone, labels, before, after):
    members, fields, local_rows, size = everyone.shape
    rows = fields * local_rows * size // TILE + REGIONS
    return pl.pallas_call(
        pair_kernel,
        out_shape=jax.ShapeDtypeStruct((members, rows, TILE), jnp.float32),
        in_specs=[SMEM, SMEM, VMEM, VMEM, VMEM, VMEM],
        out_specs=VMEM,
        scratch_shapes=[pltpu.VMEM((local_rows + 2 * STRIP, TILE), jnp.float32)],
        compiler_params=pltpu.CompilerParams(vmem_limit_bytes=6 << 20),
        cost_estimate=pl.CostEstimate(flops=1 << 20, bytes_accessed=3 << 20, transcendentals=0),
        name="pair_spread",
    )(where, pairing, everyone, labels, before, after)


def spread_edge_kernel(shape, back_ref, up_ref, down_ref, share_ref):
    fields, local_rows, width = shape
    chunks = back_ref.shape[0]
    tiles = width // chunks // TILE
    tail = fields * tiles * local_rows
    share = back_ref[0, tail:, :]
    for c in range(1, chunks):
        share = share + back_ref[c, tail:, :]
    for i in range(share_ref.shape[0]):
        share_ref[i] = share
    for c in range(chunks):
        for t in range(tiles):
            tile = c * tiles + t
            at = slice(tile * TILE, (tile + 1) * TILE)
            values = []
            for i in range(fields):
                row = (i * tiles + t) * local_rows
                values.append(back_ref[c, row : row + local_rows, :])
            pack_rows(up_ref, down_ref, at, *values)


def spread_edges(back, shape, lat_size):
    edge = jax.ShapeDtypeStruct((3 * STRIP, shape[2]), jnp.float32)
    return pl.pallas_call(
        functools.partial(spread_edge_kernel, shape),
        out_shape=(edge, edge, jax.ShapeDtypeStruct((lat_size, REGIONS, TILE), jnp.float32)),
        in_specs=[VMEM],
        out_specs=(VMEM,) * 3,
        compiler_params=pltpu.CompilerParams(vmem_limit_bytes=6 << 20),
        cost_estimate=pl.CostEstimate(flops=1 << 18, bytes_accessed=2 << 20, transcendentals=0),
        name="spread_edges",
    )(back)


def recentre_kernel(
    labels_ref, analysis_ref, a_before_ref, a_after_ref, back_ref, b_before_ref, b_after_ref,
    shares_ref, mid_ref, before_ref, after_ref, factor_ref
):
    chunks = back_ref.shape[0]
    fields, local_rows, width = analysis_ref.shape
    tiles = width // chunks // TILE
    sums = jnp.sum(shares_ref[...], axis=0)
    region_sum = jnp.broadcast_to(sums[:, 0:1], (REGIONS, TILE))
    cells = jnp.broadcast_to(sums[:, 1:2], (REGIONS, TILE))
    factor = target_size / jnp.sqrt(region_sum / cells + small_eps)
    diagonal = lax.broadcasted_iota(jnp.int32, factor.shape, 0) == lax.broadcasted_iota(
        jnp.int32, factor.shape, 1
    )
    in_lanes = jnp.sum(jnp.where(diagonal, factor, 0.0), axis=0, keepdims=True)
    factor_ref[...] = in_lanes[:, 0:REGIONS]

    def scale_of(labels):
        scale = jnp.zeros(labels.shape, jnp.float32)
        for r in range(REGIONS):
            scale = jnp.where(labels == float(r + 1), factor[r : r + 1, :], scale)
        return scale

    def rows_of(ref, row):
        parts = [ref[row : row + 1, k * TILE : (k + 1) * TILE] for k in range(STRIP)]
        return jnp.concatenate(parts, axis=0)

    scale = scale_of(labels_ref[...])
    below = scale_of(rows_of(a_before_ref, 8))
    above = scale_of(rows_of(a_after_ref, 15))
    row = lax.broadcasted_iota(jnp.int32, (STRIP, TILE), 0)
    below_uq = jnp.where(row < 3, pltpu.roll(below, 3, 0), below)
    above_uq = jnp.where(row >= 5, pltpu.roll(above, 5, 0), above)

    for c in range(chunks):
        for t in range(tiles):
            tile = c * tiles + t
            at = slice(tile * TILE, (tile + 1) * TILE)

            def wide(x):
                return jnp.broadcast_to(x[:, tile : tile + 1], (x.shape[0], TILE))

            own = wide(scale)
            for i in range(fields):
                first = (i * tiles + t) * local_rows
                mid_ref[i, :, at] = (
                    analysis_ref[i, :, at] + own * back_ref[c, first : first + local_rows, :]
                )
            for out, a_ref, b_ref, near, mixed in (
                (before_ref, a_before_ref, b_before_ref, below, below_uq),
                (after_ref, a_after_ref, b_after_ref, above, above_uq),
            ):
                near = wide(near)
                for rows, factor_rows in ((0, near), (8, near), (16, wide(mixed))):
                    pack = slice(rows, rows + STRIP)
                    out[pack, at] = a_ref[pack, at] + factor_rows * b_ref[pack, at]


def recentre(labels, analysis, a_before, a_after, back, b_before, b_after, shares):
    edge = jax.ShapeDtypeStruct(a_before.shape, jnp.float32)
    return pl.pallas_call(
        recentre_kernel,
        out_shape=(
            jax.ShapeDtypeStruct(analysis.shape, jnp.float32),
            edge,
            edge,
            jax.ShapeDtypeStruct((1, REGIONS), jnp.float32),
        ),
        in_specs=[VMEM] * 8,
        out_specs=(VMEM,) * 4,
        compiler_params=pltpu.CompilerParams(vmem_limit_bytes=6 << 20),
        cost_estimate=pl.CostEstimate(flops=1 << 20, bytes_accessed=4 << 20, transcendentals=0),
        name="recentre",
    )(labels, analysis, a_before, a_after, back, b_before, b_after, shares)


def local(replica_variables, analysis, labels, pairing):
    members = lax.axis_size("mem")
    lat_size = lax.axis_size("lat")
    lat = lax.axis_index("lat")
    member = lax.axis_index("mem")
    x = replica_variables[0]
    fields, local_rows, width = x.shape
    total_rows = float(local_rows * lat_size)
    where = jnp.stack([lat, jnp.int32(lat_size - 1), member]).astype(jnp.int32)
    up = [(i, i + 1) for i in range(lat_size - 1)]
    down = [(j, i) for i, j in up]

    last, first, coded = first_edges(x, labels)
    before = lax.ppermute(last, "lat", up)
    after = lax.ppermute(first, "lat", down)
    last, first = packed_edges(analysis, coded, before)
    a_before = lax.ppermute(last, "lat", up)
    a_after = lax.ppermute(first, "lat", down)
    pieces = flow(where, x, before, after, total_rows, members, "first_flow")
    everyone = lax.all_to_all(pieces, "mem", 0, 0, tiled=True)

    spread = pair_spread(where, pairing, everyone, coded, before, after)
    back = lax.all_to_all(spread, "mem", 0, 0, tiled=True)
    last, first, share = spread_edges(back, x.shape, lat_size)
    b_before = lax.ppermute(last, "lat", up)
    b_after = lax.ppermute(first, "lat", down)
    shares = lax.all_to_all(share, "lat", 0, 0, tiled=True)
    middle, before, after, factor = recentre(
        coded, analysis, a_before, a_after, back, b_before, b_after, shares
    )
    closing = flow(where, middle, before, after, total_rows, 1, "closing_flow")
    return closing[None], factor


def solution(mesh):
    return jax.shard_map(
        local,
        mesh=mesh,
        in_specs=(P("mem", None, "lat", None), P(None, "lat", None), P("lat", None), P()),
        out_specs=(P("mem", None, "lat", None), P("mem", None)),
        check_vma=False,
    )
```

```python
import functools

import jax
import jax.numpy as jnp
from jax import lax
from jax.experimental import pallas as pl
from jax.experimental.pallas import tpu as pltpu
from jax.sharding import PartitionSpec as P

TILE = 128
REGIONS = 8
STEPS = 3
STRIP = 8
PARTS = 8

grav_coef = 0.1
depth_coef = 0.1
advect_coef = 0.05
diffuse_coef = 0.05
coriolis_coef = 0.05
target_size = 0.5
small_eps = 1e-06

VMEM = pl.BlockSpec(memory_space=pltpu.VMEM)
SMEM = pl.BlockSpec(memory_space=pltpu.SMEM)


def east(field):
    return pltpu.roll(field, field.shape[1] - 1, 1)


def west(field):
    return pltpu.roll(field, 1, 1)


def pack_rows(up_ref, down_ref, at, h, u, v, q):
    row = lax.broadcasted_iota(jnp.int32, (STRIP, v.shape[1]), 0)
    up_ref[0:8, at] = v[8:16]
    up_ref[8:16, at] = h[8:16]
    up_ref[16:24, at] = jnp.where(row < 3, pltpu.roll(q[8:16], 3, 0), u[8:16])
    down_ref[0:8, at] = v[0:8]
    down_ref[8:16, at] = h[0:8]
    down_ref[16:24, at] = jnp.where(row >= 5, pltpu.roll(q[0:8], 5, 0), u[0:8])


def first_edge_kernel(fields_ref, labels_ref, up_ref, down_ref, coded_ref):
    width = fields_ref.shape[2]
    size = width // PARTS
    for c in range(PARTS):
        at = slice(c * size, (c + 1) * size)
        pack_rows(up_ref, down_ref, at, *[fields_ref[i, :, at] for i in range(4)])
    local_rows, columns = labels_ref.shape
    coded_ref[...] = jnp.zeros(coded_ref.shape, jnp.float32)
    coded_ref[:, 0:columns] = labels_ref[...].astype(jnp.float32) + 1.0
    up_ref[8:9, 0:TILE] = coded_ref[local_rows - 1 :, :]
    down_ref[15:16, 0:TILE] = coded_ref[0:1, :]


def first_edges(fields, labels):
    edge = jax.ShapeDtypeStruct((3 * STRIP, fields.shape[2]), jnp.float32)
    return pl.pallas_call(
        first_edge_kernel,
        out_shape=(edge, edge, jax.ShapeDtypeStruct((labels.shape[0], TILE), jnp.float32)),
        in_specs=[VMEM] * 2,
        out_specs=(VMEM,) * 3,
        compiler_params=pltpu.CompilerParams(vmem_limit_bytes=8 << 20),
        cost_estimate=pl.CostEstimate(flops=1 << 18, bytes_accessed=2 << 20, transcendentals=0),
        name="first_edges",
    )(fields, labels)


def edge_kernel(fields_ref, labels_ref, after_ref, up_ref, down_ref):
    width = fields_ref.shape[2]
    size = width // PARTS
    for c in range(PARTS):
        at = slice(c * size, (c + 1) * size)
        pack_rows(up_ref, down_ref, at, *[fields_ref[i, :, at] for i in range(4)])
    for k in range(STRIP):
        at = slice(k * TILE, (k + 1) * TILE)
        row = labels_ref.shape[0] - STRIP + k
        up_ref[8:9, at] = labels_ref[row : row + 1, :]
        down_ref[15:16, at] = labels_ref[k : k + 1, :]


def packed_edges(fields, labels, after):
    edge = jax.ShapeDtypeStruct((3 * STRIP, fields.shape[2]), jnp.float32)
    return pl.pallas_call(
        edge_kernel,
        out_shape=(edge, edge),
        in_specs=[VMEM, VMEM, pl.BlockSpec(memory_space=pl.ANY)],
        out_specs=(VMEM, VMEM),
        compiler_params=pltpu.CompilerParams(vmem_limit_bytes=8 << 20),
        cost_estimate=pl.CostEstimate(flops=1 << 18, bytes_accessed=2 << 20, transcendentals=0),
        name="analysis_edges",
    )(fields, labels, after)


def flow_kernel(total_rows, chunks, where_ref, mid_ref, before_ref, after_ref, out_ref, *state):
    hs, us, vs, qs, h1s = state
    lat = where_ref[0]
    last = where_ref[1]
    local_rows = mid_ref.shape[1]
    width = mid_ref.shape[2]
    strips = local_rows // STRIP + 2
    pad = STRIP

    def rows(s, shift=0):
        return pl.ds(pad + STRIP * s + shift, STRIP)

    zero = jnp.zeros((STRIP, width), jnp.float32)
    for ref in (hs, us, vs, qs, h1s):
        ref[0:pad, :] = zero
        ref[pad + STRIP * strips :, :] = zero
    for ref, field in ((hs, 0), (us, 1), (vs, 2), (qs, 3)):
        ref[pad + STRIP : pad + STRIP * (strips - 1), :] = mid_ref[field]
    for s, edge in ((0, before_ref), (strips - 1, after_ref)):
        vs[rows(s), :] = edge[0:8, :]
        hs[rows(s), :] = edge[8:16, :]
        us[rows(s), :] = edge[16:24, :]
    qs[rows(0), :] = pltpu.roll(before_ref[16:24, :], 5, 0)
    qs[rows(strips - 1), :] = pltpu.roll(after_ref[16:24, :], 3, 0)

    inside = [None] * strips
    inside[0] = jnp.where(lat > 0, 1.0, 0.0).astype(jnp.float32)
    inside[-1] = jnp.where(lat < last, 1.0, 0.0).astype(jnp.float32)

    def kept(value, s):
        return value if inside[s] is None else value * inside[s]

    lane_rows = lax.broadcasted_iota(jnp.int32, (STRIP, width), 0)

    def coriolis(s):
        row = (lane_rows + (lat * local_rows + STRIP * (s - 1))).astype(jnp.float32)
        return coriolis_coef * (2.0 * (row + 0.5) / total_rows - 1.0)

    for k in range(STEPS):
        final = k == STEPS - 1
        for s in range(strips):
            u = us[rows(s), :]
            h1s[rows(s), :] = kept(
                hs[rows(s), :]
                - depth_coef
                * ((east(u) - west(u)) + (vs[rows(s, 1), :] - vs[rows(s, -1), :])),
                s,
            )
        carried = qs[rows(0, -1), :]
        for s in range(1, strips - 1) if final else range(strips):
            f = coriolis(s)
            h1 = h1s[rows(s), :]
            v = vs[rows(s), :]
            u1 = us[rows(s), :] + f * v - grav_coef * (east(h1) - west(h1))
            v1 = v - f * u1 - grav_coef * (h1s[rows(s, 1), :] - h1s[rows(s, -1), :])
            q = qs[rows(s), :]
            if final:
                south = qs[rows(s, -1), :]
            else:
                south = carried
                if s < strips - 1:
                    carried = qs[rows(s + 1, -1), :]
            north = qs[rows(s, 1), :]
            e, w = east(q), west(q)
            q1 = (
                q
                - advect_coef * (u1 * (e - w) + v1 * (north - south))
                + diffuse_coef * ((e + w) + (north + south) - 4.0 * q)
            )
            if not final:
                us[rows(s), :] = kept(u1, s)
                vs[rows(s), :] = kept(v1, s)
                qs[rows(s), :] = kept(q1, s)
                hs[rows(s), :] = h1
            else:
                at = slice(STRIP * (s - 1), STRIP * s)
                for field, value in enumerate((h1, u1, v1, q1)):
                    if chunks == 1:
                        out_ref[field, at, :] = value
                    else:
                        size = width // chunks
                        for c in range(chunks):
                            out_ref[c, field, at, :] = value[:, c * size : (c + 1) * size]


def flow(where, middle, before, after, total_rows, chunks, name):
    fields, local_rows, width = middle.shape
    shape = (fields, local_rows, width)
    if chunks > 1:
        shape = (chunks, fields, local_rows, width // chunks)
    state = pltpu.VMEM((local_rows + 4 * STRIP, width), jnp.float32)
    return pl.pallas_call(
        functools.partial(flow_kernel, total_rows, chunks),
        out_shape=jax.ShapeDtypeStruct(shape, jnp.float32),
        in_specs=[SMEM, VMEM, VMEM, VMEM],
        out_specs=VMEM,
        scratch_shapes=[state] * 5,
        compiler_params=pltpu.CompilerParams(vmem_limit_bytes=24 << 20),
        cost_estimate=pl.CostEstimate(
            flops=60 * 10 * STRIP * width, bytes_accessed=1 << 22, transcendentals=0
        ),
        name=name,
    )(where, middle, before, after)


def pair_kernel(
    where_ref, pairing_ref, all_ref, labels_ref, before_ref, after_ref, out_hbm, near_ref,
    spread_ref, sems
):
    members, fields, local_rows, size = all_ref.shape
    tiles = size // TILE
    lane = lax.broadcasted_iota(jnp.int32, (REGIONS, TILE), 1)

    def folded(x):
        return x[:STRIP] + x[STRIP:]

    weights, counts = [], []
    near_ref[0:STRIP, :] = jnp.broadcast_to(before_ref[8:9, 0:TILE], (STRIP, TILE))
    near_ref[STRIP : STRIP + local_rows, :] = labels_ref[...]
    near_ref[STRIP + local_rows :, :] = jnp.broadcast_to(after_ref[15:16, 0:TILE], (STRIP, TILE))
    column_of = lax.broadcasted_iota(jnp.int32, (local_rows, TILE), 1)
    shown = []
    for i in range(3):
        near = near_ref[STRIP - 1 + i : STRIP - 1 + i + local_rows, :]
        shown.append([])
        for t in range(tiles):
            own = jnp.where(column_of == where_ref[2] * tiles + t, near, 0.0)
            own = jnp.sum(own, axis=1, keepdims=True)
            shown[-1].append(jnp.broadcast_to(own, (local_rows, TILE)))
    for r in range(REGIONS):

        def is_r(x):
            return jnp.where(x == float(r + 1), 1.0, 0.0).astype(jnp.float32)

        count, weight = None, []
        for t in range(tiles):
            own = is_r(shown[1][t])
            count = folded(own) if count is None else count + folded(own)
            weight.append(0.125 * (is_r(shown[0][t]) + 2.0 * own + is_r(shown[2][t])))
        counts.append(jnp.sum(count, axis=0, keepdims=True))
        weights.append(weight)

    def column(rows):
        return jnp.sum(jnp.concatenate(rows, axis=0), axis=1, keepdims=True)

    empty = jnp.where(lane == 1, column(counts), 0.0)
    copies = []
    for m in range(members):
        partner = pairing_ref[m]
        squares = [None] * tiles
        for field in range(fields):
            spread = 0.5 * (all_ref[m, field] - all_ref[partner, field])
            for t in range(tiles):
                x = spread[:, t * TILE : (t + 1) * TILE]
                at = (field * tiles + t) * local_rows
                spread_ref[m, at : at + local_rows, :] = x
                squares[t] = x * x if squares[t] is None else squares[t] + x * x
        parts = []
        for weight in weights:
            part = None
            for t in range(tiles):
                y = folded(squares[t] * weight[t])
                part = y if part is None else part + y
            parts.append(jnp.sum(part, axis=0, keepdims=True))
        spread_ref[m, fields * tiles * local_rows :, :] = jnp.where(
            lane == 0, column(parts), empty
        )
        copies.append(pltpu.make_async_copy(spread_ref.at[m], out_hbm.at[m], sems.at[m]))
        copies[m].start()
    for copy in copies:
        copy.wait()


def pair_spread(where, pairing, everyone, labels, before, after):
    members, fields, local_rows, size = everyone.shape
    rows = fields * local_rows * size // TILE + REGIONS
    return pl.pallas_call(
        pair_kernel,
        out_shape=jax.ShapeDtypeStruct((members, rows, TILE), jnp.float32),
        in_specs=[SMEM, SMEM, VMEM, VMEM, VMEM, VMEM],
        out_specs=pl.BlockSpec(memory_space=pltpu.MemorySpace.HBM),
        scratch_shapes=[
            pltpu.VMEM((local_rows + 2 * STRIP, TILE), jnp.float32),
            pltpu.VMEM((members, rows, TILE), jnp.float32),
            pltpu.SemaphoreType.DMA((members,)),
        ],
        compiler_params=pltpu.CompilerParams(vmem_limit_bytes=8 << 20),
        cost_estimate=pl.CostEstimate(flops=1 << 20, bytes_accessed=3 << 20, transcendentals=0),
        name="pair_spread",
    )(where, pairing, everyone, labels, before, after)


def spread_edge_kernel(shape, back_ref, up_ref, down_ref, share_ref):
    fields, local_rows, width = shape
    chunks = back_ref.shape[0]
    tiles = width // chunks // TILE
    tail = fields * tiles * local_rows
    share = back_ref[0, tail:, :]
    for c in range(1, chunks):
        share = share + back_ref[c, tail:, :]
    for i in range(share_ref.shape[0]):
        share_ref[i] = share
    for c in range(chunks):
        for t in range(tiles):
            tile = c * tiles + t
            at = slice(tile * TILE, (tile + 1) * TILE)
            values = []
            for i in range(fields):
                row = (i * tiles + t) * local_rows
                values.append(back_ref[c, row : row + local_rows, :])
            pack_rows(up_ref, down_ref, at, *values)


def spread_edges(back, shape, lat_size):
    edge = jax.ShapeDtypeStruct((3 * STRIP, shape[2]), jnp.float32)
    return pl.pallas_call(
        functools.partial(spread_edge_kernel, shape),
        out_shape=(edge, edge, jax.ShapeDtypeStruct((lat_size, REGIONS, TILE), jnp.float32)),
        in_specs=[VMEM],
        out_specs=(VMEM,) * 3,
        compiler_params=pltpu.CompilerParams(vmem_limit_bytes=8 << 20),
        cost_estimate=pl.CostEstimate(flops=1 << 18, bytes_accessed=2 << 20, transcendentals=0),
        name="spread_edges",
    )(back)


def recentre_kernel(
    labels_ref, analysis_ref, a_before_ref, a_after_ref, back_ref, b_before_ref, b_after_ref,
    shares_ref, mid_ref, before_ref, after_ref, factor_ref
):
    chunks = back_ref.shape[0]
    fields, local_rows, width = analysis_ref.shape
    tiles = width // chunks // TILE
    sums = jnp.sum(shares_ref[...], axis=0)
    region_sum = jnp.broadcast_to(sums[:, 0:1], (REGIONS, TILE))
    cells = jnp.broadcast_to(sums[:, 1:2], (REGIONS, TILE))
    factor = target_size / jnp.sqrt(region_sum / cells + small_eps)
    diagonal = lax.broadcasted_iota(jnp.int32, factor.shape, 0) == lax.broadcasted_iota(
        jnp.int32, factor.shape, 1
    )
    in_lanes = jnp.sum(jnp.where(diagonal, factor, 0.0), axis=0, keepdims=True)
    factor_ref[...] = in_lanes[:, 0:REGIONS]

    def scale_of(labels):
        scale = jnp.zeros(labels.shape, jnp.float32)
        for r in range(REGIONS):
            scale = jnp.where(labels == float(r + 1), factor[r : r + 1, :], scale)
        return scale

    def rows_of(ref, row):
        parts = [ref[row : row + 1, k * TILE : (k + 1) * TILE] for k in range(STRIP)]
        return jnp.concatenate(parts, axis=0)

    scale = scale_of(labels_ref[...])
    below = scale_of(rows_of(a_before_ref, 8))
    above = scale_of(rows_of(a_after_ref, 15))
    row = lax.broadcasted_iota(jnp.int32, (STRIP, TILE), 0)
    below_uq = jnp.where(row < 3, pltpu.roll(below, 3, 0), below)
    above_uq = jnp.where(row >= 5, pltpu.roll(above, 5, 0), above)

    for c in range(chunks):
        for t in range(tiles):
            tile = c * tiles + t
            at = slice(tile * TILE, (tile + 1) * TILE)

            def wide(x):
                return jnp.broadcast_to(x[:, tile : tile + 1], (x.shape[0], TILE))

            own = wide(scale)
            for i in range(fields):
                first = (i * tiles + t) * local_rows
                mid_ref[i, :, at] = (
                    analysis_ref[i, :, at] + own * back_ref[c, first : first + local_rows, :]
                )
            for out, a_ref, b_ref, near, mixed in (
                (before_ref, a_before_ref, b_before_ref, below, below_uq),
                (after_ref, a_after_ref, b_after_ref, above, above_uq),
            ):
                near = wide(near)
                for rows, factor_rows in ((0, near), (8, near), (16, wide(mixed))):
                    pack = slice(rows, rows + STRIP)
                    out[pack, at] = a_ref[pack, at] + factor_rows * b_ref[pack, at]


def recentre(labels, analysis, a_before, a_after, back, b_before, b_after, shares):
    edge = jax.ShapeDtypeStruct(a_before.shape, jnp.float32)
    return pl.pallas_call(
        recentre_kernel,
        out_shape=(
            jax.ShapeDtypeStruct(analysis.shape, jnp.float32),
            edge,
            edge,
            jax.ShapeDtypeStruct((1, REGIONS), jnp.float32),
        ),
        in_specs=[VMEM] * 8,
        out_specs=(VMEM,) * 4,
        compiler_params=pltpu.CompilerParams(vmem_limit_bytes=16 << 20),
        cost_estimate=pl.CostEstimate(flops=1 << 20, bytes_accessed=4 << 20, transcendentals=0),
        name="recentre",
    )(labels, analysis, a_before, a_after, back, b_before, b_after, shares)


def local(replica_variables, analysis, labels, pairing):
    members = lax.axis_size("mem")
    lat_size = lax.axis_size("lat")
    lat = lax.axis_index("lat")
    member = lax.axis_index("mem")
    x = replica_variables[0]
    fields, local_rows, width = x.shape
    total_rows = float(local_rows * lat_size)
    where = jnp.stack([lat, jnp.int32(lat_size - 1), member]).astype(jnp.int32)
    up = [(i, i + 1) for i in range(lat_size - 1)]
    down = [(j, i) for i, j in up]

    last, first, coded = first_edges(x, labels)
    before = lax.ppermute(last, "lat", up)
    after = lax.ppermute(first, "lat", down)
    last, first = packed_edges(analysis, coded, before)
    a_before = lax.ppermute(last, "lat", up)
    a_after = lax.ppermute(first, "lat", down)
    pieces = flow(where, x, before, after, total_rows, members, "first_flow")
    everyone = lax.all_to_all(pieces, "mem", 0, 0, tiled=True)

    spread = pair_spread(where, pairing, everyone, coded, before, after)
    back = lax.all_to_all(spread, "mem", 0, 0, tiled=True)
    last, first, share = spread_edges(back, x.shape, lat_size)
    b_before = lax.ppermute(last, "lat", up)
    b_after = lax.ppermute(first, "lat", down)
    shares = lax.all_to_all(share, "lat", 0, 0, tiled=True)
    middle, before, after, factor = recentre(
        coded, analysis, a_before, a_after, back, b_before, b_after, shares
    )
    closing = flow(where, middle, before, after, total_rows, 1, "closing_flow")
    return closing[None], factor


def solution(mesh):
    return jax.shard_map(
        local,
        mesh=mesh,
        in_specs=(P("mem", None, "lat", None), P(None, "lat", None), P("lat", None), P()),
        out_specs=(P("mem", None, "lat", None), P("mem", None)),
        check_vma=False,
    )
```
